512 devices in a mesh: prow: 16 (over y, core), pcol: 32 (over z, x).
Axes of the slice: x: 4, y: 8, z: 8, core: 2. Of those that a mesh axis runs over, the one named last changes fastest.
Arguments:
- embeddings: bfloat16 [12, 16, 128, 768], P(None, 'prow', None, 'pcol'), may hold values from -6 to 6
- noise_var: bfloat16 [12, 16, 128], P(None, 'prow'), may hold values from 0.5 to 2
Outputs:
- schur_block: float32 [12, 16, 128, 6, 32, 128], P(None, 'prow', None, None, 'pcol')
- panel_cols: float32 [12, 16, 128, 128], P(None, 'prow', 'pcol')
The draws below stay inside these ranges and needn't reach their ends.
All inputs are finite; a program needn't handle non-finite values.
Results may differ from the reference program's by a relative error of at most 0.0003.
Values may be sent and summed in bfloat16 or wider, within the bound.
A program may use at most 64 MiB of HBM per device.

```python
import math
import jax
import jax.numpy as jnp
from jax import lax

E = 768
N = 24576
TILE = 128
TILES = 192
N_PROW = 16
N_PCOL = 32


def level_of(rng, extent, shards, low, largest):
    factor_of = 1.0
    for dim, blocks in shards:
        heights = jax.random.uniform(jax.random.fold_in(jax.random.fold_in(rng, 6), dim), (blocks,), jnp.float32, low / len(shards), largest / len(shards))
        factor_of = factor_of * jnp.repeat(jnp.exp(heights), extent[dim] // blocks).reshape((-1,) + (1,) * (len(extent) - 1 - dim))
    return factor_of


def scatter_about(key, dims, width, most, cuts=(), kind=jnp.bfloat16):
    array = width * jax.random.normal(key, dims, jnp.float32)
    if cuts:
        array = array * level_of(key, dims, cuts, -0.22, 0.18)
    return jnp.clip(array, -most, most).astype(kind)


def setup_inputs(seed: int = 0) -> dict:
    keys = jax.random.split(jax.random.key(seed), 3)
    return {
        "embeddings": scatter_about(keys[0], (TILES // N_PROW, N_PROW, TILE, E), 1.0, 6.0, ((1, 16), (3, 32))),
        "noise_var": jnp.clip(jnp.exp(math.log(2.0) - 1.3862944 * jax.random.uniform(keys[1], (TILES // N_PROW, N_PROW, TILE), jnp.float32) ** level_of(keys[1], (TILES // N_PROW, N_PROW, TILE), ((1, 16),), -0.2, 0.2)), 0.5, 2.0).astype(jnp.bfloat16),
    }


def squares(values):
    return jnp.sum(jnp.square(values.astype(jnp.float32)), axis=-1)

def kernel_block(left_x, right_x, left_sq, right_sq):
    inner_dots = jnp.dot(left_x.astype(jnp.float32), right_x.T.astype(jnp.float32), preferred_element_type=jnp.float32)
    return jnp.exp(-(left_sq[:, None] + right_sq[None, :] - 2.0 * inner_dots) / E)

def reference(embeddings, noise_var):
    all_rows = embeddings.reshape(N, E)
    variance = noise_var.reshape(N).astype(jnp.float32)
    all_sq = squares(all_rows)
    first_x = all_rows[:TILE]
    row_ids = jnp.arange(N, dtype=jnp.int32)
    tile_ids = jnp.arange(TILE, dtype=jnp.int32)
    first_kernel = kernel_block(all_rows, first_x, all_sq, all_sq[:TILE])
    first_kernel = first_kernel + jnp.where(row_ids[:, None] == tile_ids[None, :], variance[:TILE][None, :], jnp.float32(0.0))
    factor = jnp.linalg.cholesky(first_kernel[:TILE])
    panel_full = lax.linalg.triangular_solve(factor, first_kernel, left_side=False, lower=True, transpose_a=True)

    def one_block(packed):
        rows_x, rows_sq, rows_var, rows_panel, block_start = packed
        kernel_rows = kernel_block(rows_x, all_rows, rows_sq, all_sq)
        own_ids = block_start + tile_ids
        on_diagonal = jnp.where(row_ids[None, :] == own_ids[:, None], rows_var[:, None], jnp.float32(0.0))
        update = jnp.dot(rows_panel.astype(jnp.float32), panel_full.T.astype(jnp.float32), precision=lax.Precision.HIGHEST, preferred_element_type=jnp.float32)
        return kernel_rows + on_diagonal - update
    starts = (jnp.arange(TILES, dtype=jnp.int32) * TILE).astype(jnp.int32)
    stacked = lax.map(one_block, (all_rows.reshape(TILES, TILE, E), all_sq.reshape(TILES, TILE), variance.reshape(TILES, TILE), panel_full.reshape(TILES, TILE, TILE), starts))
    schur_block = stacked.reshape(TILES // N_PROW, N_PROW, TILE, TILES // N_PCOL, N_PCOL, TILE)
    panel_cols = panel_full.reshape(TILES // N_PROW, N_PROW, TILE, TILE)
    return (schur_block, panel_cols)
```

```python
import functools

import jax
import jax.numpy as jnp
from jax import lax
from jax.experimental import pallas as pl
from jax.experimental.pallas import tpu as pltpu
from jax.sharding import PartitionSpec as P

F32 = jnp.float32
BF16 = jnp.bfloat16


def from_root(value, axis, source):
    kept = jnp.where(lax.axis_index(axis) == source, value, 0).astype(value.dtype)
    return lax.psum(kept, axis)


def feature_squares(block):
    wide = block.astype(F32)
    return jnp.sum(wide * wide, axis=0, keepdims=True)


def down(row):
    tile = row.shape[1]
    return jnp.transpose(jnp.broadcast_to(row, (tile, tile)))


def eye_mask(tile):
    rows = lax.broadcasted_iota(jnp.int32, (tile, tile), 0)
    cols = lax.broadcasted_iota(jnp.int32, (tile, tile), 1)
    return rows == cols


def split3(panel, left):
    high = panel.astype(BF16)
    low = (panel - high.astype(F32)).astype(BF16)
    return jnp.concatenate([high, high, low] if left else [high, low, high], axis=1)


def matmul(left, right):
    return lax.dot_general(left, right, (((1,), (0,)), ((), ())), preferred_element_type=F32)


def matmul_nt(left, right, precision=None):
    return lax.dot_general(
        left, right, (((1,), (1,)), ((), ())), precision=precision, preferred_element_type=F32
    )


def inverse_factor(first, noise, work):
    feats, tile = first.shape
    sq = feature_squares(first)
    dots = matmul(jnp.transpose(first), first)
    gram = jnp.exp((2.0 * dots - (down(sq) + sq)) * (1.0 / feats))
    diagonal = eye_mask(tile)
    work[...] = gram + jnp.where(diagonal, noise, 0.0)
    part = tile // 4
    for base in range(0, tile, part):
        height = tile - base
        lanes = lax.broadcasted_iota(jnp.int32, (height, tile), 1)
        ids = lax.broadcasted_iota(jnp.int32, (height, tile), 0) + base

        def step(k, carry, base=base, lanes=lanes, ids=ids):
            held = work[base:, :]
            at_k = lanes == k
            pivot = work[pl.ds(k, 1), :]
            here = at_k[:1]
            inv = 1.0 / jnp.sum(jnp.where(here, pivot, 0.0), axis=1, keepdims=True)
            column = jnp.sum(jnp.where(at_k, held, 0.0), axis=1, keepdims=True)
            scaled = jnp.where(here, 1.0, pivot) * inv
            factor = jnp.where(ids > k, column, 0.0)
            cleared = jnp.where(at_k & (ids > k), 0.0, held)
            work[base:, :] = cleared - factor * scaled
            return carry

        lax.fori_loop(base, base + part, step, 0)
    done = work[...]
    pivots = jnp.sum(jnp.where(diagonal, done, 0.0), axis=1, keepdims=True)
    rows = lax.broadcasted_iota(jnp.int32, (tile, tile), 0)
    cols = lax.broadcasted_iota(jnp.int32, (tile, tile), 1)
    unit = jnp.where(cols < rows, done, jnp.where(diagonal, 1.0, 0.0))
    return unit * (1.0 / jnp.sqrt(pivots))


def factor_kernel(first_ref, noise_ref, inverse_ref, work):
    inverse_ref[...] = inverse_factor(first_ref[...], noise_ref[...], work)


def schur_kernel(
    row_count, col_count, row_ref, col_ref, first_ref, noise_ref, inverse_ref,
    schur_ref, share_ref, wide, col_sq, col_panel, panel,
):
    step = pl.program_id(0)
    group, feats, tile = row_ref.shape
    col_tiles = col_ref.shape[0]
    scale = 1.0 / feats
    r, q = lax.axis_index("prow"), lax.axis_index("pcol")
    diagonal = eye_mask(tile)
    first = first_ref[...]
    first_sq = feature_squares(first)
    inverse = inverse_ref[...]

    def panel_of(samples, sq, noise, is_first):
        gram = jnp.exp((2.0 * matmul(samples, first) - (sq + first_sq)) * scale)
        gram = gram + jnp.where(diagonal & is_first, noise, 0.0)
        return matmul_nt(gram, inverse, lax.Precision.HIGHEST)

    @pl.when(step == 0)
    def _():
        for d in range(col_tiles):
            block = col_ref[d]
            place = slice(d * tile, (d + 1) * tile)
            wide[:, place] = block
            sq = feature_squares(block)
            col_sq[:, place] = sq
            noise = noise_ref[noise_ref.shape[0] - 1 :, :]
            is_first = (q == 0) if d == 0 else False
            col_panel[place, :] = split3(
                panel_of(jnp.transpose(block), down(sq), noise, is_first), False
            )

    stride = col_tiles
    share = tile // col_count
    shares = []
    for t in range(group):
        a = step * group + t
        block = row_ref[t]
        samples = jnp.transpose(block)
        sq = down(feature_squares(block))
        noise = noise_ref[pl.ds(a, 1), :]
        rows = panel_of(samples, sq, noise, a * row_count + r == 0)
        panel[t * tile : (t + 1) * tile, :] = rows
        dots = matmul(samples, wide[...])
        update = matmul_nt(split3(rows, True), col_panel[...])
        for d in range(col_tiles):
            place = slice(d * tile, (d + 1) * tile)
            gram = jnp.exp((2.0 * dots[:, place] - (sq + col_sq[:, place])) * scale)
            same = a * row_count + r == d * col_count + q
            gram = gram + jnp.where(diagonal & same, noise, 0.0)
            schur_ref[pl.ds(t * tile * stride + d, tile, stride=stride), :] = gram - update[:, place]
        shares.append(panel[pl.ds(t * tile + q * share, share), :])
    share_ref[...] = jnp.concatenate(shares, axis=0)


def shards(embeddings, noise_var):
    row_count, col_count = lax.axis_size("prow"), lax.axis_size("pcol")
    col_index = lax.axis_index("pcol")
    local = jnp.transpose(embeddings[:, 0], (0, 2, 1))
    rows = lax.all_gather(local, "pcol", axis=1, tiled=True)
    row_tiles, feats, tile = rows.shape
    col_tiles = row_tiles * row_count // col_count
    ratio = col_count // row_count
    first, first_noise = from_root(rows[0], "prow", 0), from_root(noise_var[0, 0], "prow", 0)
    chosen = lax.dynamic_index_in_dim(
        rows.reshape(col_tiles, ratio, feats, tile), col_index // row_count, 1, keepdims=False
    )
    cols = from_root(chosen, "prow", col_index % row_count)
    return finish(rows, cols, first, noise_var, first_noise)


def finish(rows, cols, first, noise_var, first_noise):
    row_count, col_count = lax.axis_size("prow"), lax.axis_size("pcol")
    row_tiles, feats, tile = rows.shape
    col_tiles = cols.shape[0]
    noise = jnp.concatenate([noise_var[:, 0], first_noise[None]], axis=0).astype(F32)
    inverse = pl.pallas_call(
        factor_kernel,
        out_shape=jax.ShapeDtypeStruct((tile, tile), F32),
        scratch_shapes=[pltpu.VMEM((tile, tile), F32)],
        name="factor",
    )(first, noise[row_tiles:])
    group = 2
    share = tile // col_count
    height = group * tile * col_tiles
    schur, shared = pl.pallas_call(
        functools.partial(schur_kernel, row_count, col_count),
        grid=(row_tiles // group,),
        in_specs=[
            pl.BlockSpec((group, feats, tile), lambda i: (i, 0, 0)),
            pl.BlockSpec((col_tiles, feats, tile), lambda i: (0, 0, 0)),
            pl.BlockSpec((feats, tile), lambda i: (0, 0)),
            pl.BlockSpec((row_tiles + 1, tile), lambda i: (0, 0)),
            pl.BlockSpec((tile, tile), lambda i: (0, 0)),
        ],
        out_specs=[
            pl.BlockSpec((height, tile), lambda i: (i, 0)),
            pl.BlockSpec((group * share, tile), lambda i: (i, 0)),
        ],
        out_shape=[
            jax.ShapeDtypeStruct((row_tiles * tile * col_tiles, tile), F32),
            jax.ShapeDtypeStruct((row_tiles * share, tile), F32),
        ],
        scratch_shapes=[
            pltpu.VMEM((feats, col_tiles * tile), BF16),
            pltpu.VMEM((1, col_tiles * tile), F32),
            pltpu.VMEM((col_tiles * tile, 3 * tile), BF16),
            pltpu.VMEM((group * tile, tile), F32),
        ],
        name="schur",
    )(rows, cols, first, noise, inverse)
    return (
        schur.reshape(row_tiles, 1, tile, col_tiles, 1, tile),
        shared.reshape(row_tiles, 1, share, tile),
    )


def solution(mesh):
    placed = (P(None, "prow", None, "pcol"), P(None, "prow", None))
    return jax.shard_map(
        shards,
        mesh=mesh,
        in_specs=placed,
        out_specs=(P(None, "prow", None, None, "pcol", None), P(None, "prow", "pcol", None)),
        check_vma=False,
    )
```

```python
import functools

import jax
import jax.numpy as jnp
from jax import lax
from jax.experimental import pallas as pl
from jax.experimental.pallas import tpu as pltpu
from jax.sharding import PartitionSpec as P

F32 = jnp.float32
BF16 = jnp.bfloat16


def feature_squares(block):
    wide = block.astype(F32)
    return jnp.sum(wide * wide, axis=0, keepdims=True)


def down(row):
    tile = row.shape[1]
    return jnp.transpose(jnp.broadcast_to(row, (tile, tile)))


def eye_mask(tile):
    rows = lax.broadcasted_iota(jnp.int32, (tile, tile), 0)
    cols = lax.broadcasted_iota(jnp.int32, (tile, tile), 1)
    return rows == cols


def split3(panel, left):
    high = panel.astype(BF16)
    low = (panel - high.astype(F32)).astype(BF16)
    return jnp.concatenate([high, high, low] if left else [high, low, high], axis=1)


def matmul(left, right):
    return lax.dot_general(left, right, (((1,), (0,)), ((), ())), preferred_element_type=F32)


def matmul_nt(left, right, precision=None):
    return lax.dot_general(
        left, right, (((1,), (1,)), ((), ())), precision=precision, preferred_element_type=F32
    )


def inverse_factor(first, noise, work):
    feats, tile = first.shape
    sq = feature_squares(first)
    dots = matmul(jnp.transpose(first), first)
    gram = jnp.exp((2.0 * dots - (down(sq) + sq)) * (1.0 / feats))
    diagonal = eye_mask(tile)
    work[...] = gram + jnp.where(diagonal, noise, 0.0)
    part = tile // 4
    for base in range(0, tile, part):
        height = tile - base
        lanes = lax.broadcasted_iota(jnp.int32, (height, tile), 1)
        ids = lax.broadcasted_iota(jnp.int32, (height, tile), 0) + base

        def step(k, carry, base=base, lanes=lanes, ids=ids):
            held = work[base:, :]
            at_k = lanes == k
            pivot = work[pl.ds(k, 1), :]
            here = at_k[:1]
            inv = 1.0 / jnp.sum(jnp.where(here, pivot, 0.0), axis=1, keepdims=True)
            column = jnp.sum(jnp.where(at_k, held, 0.0), axis=1, keepdims=True)
            scaled = jnp.where(here, 1.0, pivot) * inv
            factor = jnp.where(ids > k, column, 0.0)
            cleared = jnp.where(at_k & (ids > k), 0.0, held)
            work[base:, :] = cleared - factor * scaled
            return carry

        lax.fori_loop(base, base + part, step, 0)
    done = work[...]
    pivots = jnp.sum(jnp.where(diagonal, done, 0.0), axis=1, keepdims=True)
    rows = lax.broadcasted_iota(jnp.int32, (tile, tile), 0)
    cols = lax.broadcasted_iota(jnp.int32, (tile, tile), 1)
    unit = jnp.where(cols < rows, done, jnp.where(diagonal, 1.0, 0.0))
    return unit * (1.0 / jnp.sqrt(pivots))


def factor_kernel(first_ref, noise_ref, inverse_ref, work):
    inverse_ref[...] = inverse_factor(first_ref[...], noise_ref[...], work)


def schur_kernel(
    row_count, col_count, row_ref, col_ref, first_ref, noise_ref, inverse_ref,
    schur_ref, share_ref, wide, col_sq, col_panel, panel,
):
    step = pl.program_id(0)
    group, feats, tile = row_ref.shape
    col_tiles = col_ref.shape[0]
    scale = 1.0 / feats
    r, q = lax.axis_index("prow"), lax.axis_index("pcol")
    diagonal = eye_mask(tile)
    first = first_ref[...]
    first_sq = feature_squares(first)
    inverse = inverse_ref[...]

    def panel_of(samples, sq, noise, is_first):
        gram = jnp.exp((2.0 * matmul(samples, first) - (sq + first_sq)) * scale)
        gram = gram + jnp.where(diagonal & is_first, noise, 0.0)
        return matmul_nt(gram, inverse, lax.Precision.HIGHEST)

    @pl.when(step == 0)
    def _():
        for d in range(col_tiles):
            block = col_ref[d]
            place = slice(d * tile, (d + 1) * tile)
            wide[:, place] = block
            sq = feature_squares(block)
            col_sq[:, place] = sq
            noise = noise_ref[noise_ref.shape[0] - 1 :, :]
            is_first = (q == 0) if d == 0 else False
            col_panel[place, :] = split3(
                panel_of(jnp.transpose(block), down(sq), noise, is_first), False
            )

    stride = col_tiles
    share = tile // col_count
    shares = []
    for t in range(group):
        a = step * group + t
        block = row_ref[t]
        samples = jnp.transpose(block)
        sq = down(feature_squares(block))
        noise = noise_ref[pl.ds(a, 1), :]
        rows = panel_of(samples, sq, noise, a * row_count + r == 0)
        panel[t * tile : (t + 1) * tile, :] = rows
        dots = matmul(samples, wide[...])
        update = matmul_nt(split3(rows, True), col_panel[...])
        for d in range(col_tiles):
            place = slice(d * tile, (d + 1) * tile)
            gram = jnp.exp((2.0 * dots[:, place] - (sq + col_sq[:, place])) * scale)
            same = a * row_count + r == d * col_count + q
            gram = gram + jnp.where(diagonal & same, noise, 0.0)
            schur_ref[pl.ds(t * tile * stride + d, tile, stride=stride), :] = gram - update[:, place]
        shares.append(panel[pl.ds(t * tile + q * share, share), :])
    share_ref[...] = jnp.concatenate(shares, axis=0)


def gather_kernel(
    shape, local, noise, rows, cols, first, first_noise,
    held, own_sem, lead_send, lead_recv, x_send, x_recv, z_send, z_recv, y_send, y_recv, root_sem,
):
    nx, nz, ny = shape
    col_tiles, ratio = rows.shape[:2]
    half = col_tiles // 2
    r, q = lax.axis_index("prow"), lax.axis_index("pcol")
    x, z = lax.rem(q, nx), lax.div(q, nx)
    core, y = lax.rem(r, 2), lax.div(r, 2)
    prow, total = 2 * ny, nx * nz
    owner = lax.rem(q, prow)
    side = lax.div(q, prow)
    place = lax.rem(y - lax.div(owner, 2) + ny, ny)
    on_line = core == lax.rem(owner, 2)
    is_root = on_line & (place == 0)
    is_relay = on_line & (place != 0)
    is_lead = r == 0
    far = ny // 2
    goes_up = place < far
    goes_down = (place == 0) | (place > far + 1)

    def near_z(shift):
        return lax.rem(z + shift + nz, nz)

    def x_peer(k):
        return nx * z + lax.rem(x + k, nx)

    def z_peer(shift):
        return nx * near_z(shift) + x

    def y_peer(shift):
        return 2 * lax.rem(y + shift + ny, ny) + core

    def remote(src, dst, send, recv, row, col):
        return pltpu.make_async_remote_copy(
            src_ref=src, dst_ref=dst, send_sem=send, recv_sem=recv,
            device_id=(row, col), device_id_type=pl.DeviceIdType.MESH,
        )

    barrier = pltpu.get_barrier_semaphore()
    for k in range(1, prow):
        pl.semaphore_signal(
            barrier, device_id=(lax.rem(r + k, prow), q), device_id_type=pl.DeviceIdType.MESH
        )
    peers = [x_peer(k) for k in range(1, nx)] + [z_peer(1), z_peer(-1)]
    for peer in peers:
        pl.semaphore_signal(barrier, device_id=(r, peer), device_id_type=pl.DeviceIdType.MESH)
    pl.semaphore_wait(barrier, prow - 1 + len(peers))

    def lead(k):
        return [
            remote(local.at[0, 0], first.at[z, x], lead_send.at[0, k - 1], lead_recv.at[0], k, q),
            remote(noise, first_noise, lead_send.at[1, k - 1], lead_recv.at[1], k, q),
        ]

    own_lead = [
        pltpu.make_async_copy(local.at[0, 0], first.at[z, x], own_sem.at[1]),
        pltpu.make_async_copy(noise, first_noise, own_sem.at[2]),
    ]

    @pl.when(is_lead)
    def _():
        for k in range(1, prow):
            for copy in lead(k):
                copy.start()
        for copy in own_lead:
            copy.start()

    own = pltpu.make_async_copy(local, rows.at[:, :, z, x], own_sem.at[0])
    own.start()

    def part(chunk, at_z, at_x=None):
        spot = (at_z,) if at_x is None else (at_z, at_x)
        if chunk == 0:
            return first.at[spot]
        tiles = pl.ds((chunk - 1) * half, half)
        return rows.at[(tiles, slice(None), *spot)]

    def x_copy(chunk, k):
        source = part(0, z, x) if chunk == 0 else local.at[pl.ds((chunk - 1) * half, half)]
        return remote(
            source, part(chunk, z, x), x_send.at[chunk, k - 1], x_recv.at[chunk, k - 1], r, x_peer(k)
        )

    for chunk in (1, 2):
        for k in range(1, nx):
            x_copy(chunk, k).start()

    @pl.when(is_lead)
    def _():
        for copy in own_lead:
            copy.wait()

    @pl.when(jnp.logical_not(is_lead))
    def _():
        for copy in lead(1):
            copy.wait_recv()

    for k in range(1, nx):
        x_copy(0, k).start()

    last = nz // 2

    def has(way, step, chunk):
        return step < last or (chunk == 2) == (way == 1)

    def z_send_copy(way, step, chunk):
        toward = 1 if way == 0 else -1
        block = part(chunk, near_z(-toward * (step - 1)))
        return remote(
            block, block, z_send.at[way, step - 1, chunk], z_recv.at[way, step - 1, chunk],
            r, z_peer(toward),
        )

    def z_arrived(way, step, chunk):
        toward = 1 if way == 0 else -1
        block = part(chunk, near_z(-toward * step))
        remote(
            block, block, z_send.at[way, step - 1, chunk], z_recv.at[way, step - 1, chunk],
            r, z_peer(toward),
        ).wait_recv()

    def y_group(step):
        ways = (0,) if step == 0 else (0, 1)
        return [
            (step, way, piece) for piece in (0, 1) for way in ways
            if step == 0 or has(way, step, piece + 1)
        ]

    y_order = [item for step in range(last + 1) for item in y_group(step)]

    def y_place(item):
        step, way, _ = item
        return near_z(-step if way == 0 else step)

    def col_part(item):
        return cols.at[pl.ds(item[2] * half, half), y_place(item)]

    def y_copies(item, from_rows):
        i = y_order.index(item)
        tiles = pl.ds(item[2] * half, half)
        source = rows.at[tiles, side, y_place(item)] if from_rows else col_part(item)
        to = [y_peer(1), y_peer(-1), 2 * y + 1 - core]
        return [
            remote(source, col_part(item), y_send.at[i, n], y_recv.at[i], row, q)
            for n, row in enumerate(to)
        ]

    def each_way(copies, act):
        pl.when(goes_up)(lambda: act(copies[0]))
        pl.when(goes_down)(lambda: act(copies[1]))
        act(copies[2])

    def keep(item):
        i = y_order.index(item)
        tiles = pl.ds(item[2] * half, half)
        buffer = held.at[tiles, y_place(item)]
        return (
            pltpu.make_async_copy(rows.at[tiles, side, y_place(item)], buffer, root_sem.at[0, i]),
            pltpu.make_async_copy(buffer, col_part(item), root_sem.at[1, i]),
        )

    def y_start(item):
        @pl.when(is_root)
        def _():
            each_way(y_copies(item, True), lambda copy: copy.start())
            keep(item)[0].start()

    def y_relay(item):
        @pl.when(is_relay)
        def _():
            copies = y_copies(item, False)
            copies[2].wait_recv()
            each_way(copies, lambda copy: copy.start())

    for chunk in (0, 1, 2):
        if chunk == 1:
            own.wait()
        for k in range(1, nx):
            x_copy(chunk, k).wait_recv()
        for way in (0, 1):
            z_send_copy(way, 1, chunk).start()
        if chunk:
            y_start((0, 0, chunk - 1))
    lag = 2
    for step in range(2, last + 2):
        for chunk in (0, 1, 2):
            for way in (0, 1):
                if has(way, step - 1, chunk):
                    z_arrived(way, step - 1, chunk)
                    if step <= last and has(way, step, chunk):
                        z_send_copy(way, step, chunk).start()
                    if chunk:
                        y_start((step - 1, way, chunk - 1))
        if step - 1 >= lag:
            for item in y_group(step - 1 - lag):
                y_relay(item)
    for step in range(last + 1 - lag, last + 1):
        for item in y_group(step):
            y_relay(item)

    @pl.when(is_root)
    def _():
        for item in y_order:
            take, put = keep(item)
            take.wait()
            put.start()
        for item in y_order:
            keep(item)[1].wait()
            each_way(y_copies(item, True), lambda copy: copy.wait_send())

    @pl.when(is_relay)
    def _():
        for item in y_order:
            each_way(y_copies(item, False), lambda copy: copy.wait_send())

    @pl.when(jnp.logical_not(on_line))
    def _():
        for item in y_order:
            y_copies(item, False)[2].wait_recv()

    @pl.when(is_lead)
    def _():
        for k in range(1, prow):
            for copy in lead(k):
                copy.wait_send()

    for chunk in (0, 1, 2):
        for k in range(1, nx):
            x_copy(chunk, k).wait_send()
        for way in (0, 1):
            for step in range(1, last + 1):
                if has(way, step, chunk):
                    z_send_copy(way, step, chunk).wait_send()


def shards(embeddings, noise_var):
    row_count, col_count = lax.axis_size("prow"), lax.axis_size("pcol")
    nx, nz, ny = 4, col_count // 4, row_count // 2
    row_tiles, _, tile, width = embeddings.shape
    ratio = col_count // row_count
    col_tiles = row_tiles // ratio
    local = jnp.transpose(embeddings[:, 0], (0, 2, 1)).reshape(col_tiles, ratio, width, tile)
    noise = jnp.broadcast_to(noise_var[0].astype(F32), (8, tile))
    pieces = 2 * nz
    anywhere = pl.BlockSpec(memory_space=pl.ANY)
    vmem = pl.BlockSpec(memory_space=pltpu.VMEM)
    dma = pltpu.SemaphoreType.DMA
    rows, cols, first, first_noise = pl.pallas_call(
        functools.partial(gather_kernel, (nx, nz, ny)),
        in_specs=[vmem, vmem],
        out_specs=[anywhere, anywhere, anywhere, vmem],
        out_shape=[
            jax.ShapeDtypeStruct((col_tiles, ratio, nz, nx, width, tile), BF16),
            jax.ShapeDtypeStruct((col_tiles, nz, nx, width, tile), BF16),
            jax.ShapeDtypeStruct((nz, nx, width, tile), BF16),
            jax.ShapeDtypeStruct((8, tile), F32),
        ],
        scratch_shapes=[
            pltpu.VMEM((col_tiles, nz, nx, width, tile), BF16),
            dma((3,)),
            dma((2, row_count - 1)),
            dma((2,)),
            dma((3, nx - 1)),
            dma((3, nx - 1)),
            dma((2, nz // 2, 3)),
            dma((2, nz // 2, 3)),
            dma((pieces, 3)),
            dma((pieces,)),
            dma((2, pieces)),
        ],
        compiler_params=pltpu.CompilerParams(collective_id=0, has_side_effects=True),
        name="gather",
    )(local, noise)
    feats = width * col_count
    return finish(
        rows.reshape(row_tiles, feats, tile),
        cols.reshape(col_tiles, feats, tile),
        first.reshape(feats, tile),
        noise_var,
        first_noise[0],
    )


def finish(rows, cols, first, noise_var, first_noise):
    row_count, col_count = lax.axis_size("prow"), lax.axis_size("pcol")
    row_tiles, feats, tile = rows.shape
    col_tiles = cols.shape[0]
    noise = jnp.concatenate([noise_var[:, 0], first_noise[None]], axis=0).astype(F32)
    inverse = pl.pallas_call(
        factor_kernel,
        out_shape=jax.ShapeDtypeStruct((tile, tile), F32),
        scratch_shapes=[pltpu.VMEM((tile, tile), F32)],
        name="factor",
    )(first, noise[row_tiles:])
    group = 2
    share = tile // col_count
    height = group * tile * col_tiles
    schur, shared = pl.pallas_call(
        functools.partial(schur_kernel, row_count, col_count),
        grid=(row_tiles // group,),
        in_specs=[
            pl.BlockSpec((group, feats, tile), lambda i: (i, 0, 0)),
            pl.BlockSpec((col_tiles, feats, tile), lambda i: (0, 0, 0)),
            pl.BlockSpec((feats, tile), lambda i: (0, 0)),
            pl.BlockSpec((row_tiles + 1, tile), lambda i: (0, 0)),
            pl.BlockSpec((tile, tile), lambda i: (0, 0)),
        ],
        out_specs=[
            pl.BlockSpec((height, tile), lambda i: (i, 0)),
            pl.BlockSpec((group * share, tile), lambda i: (i, 0)),
        ],
        out_shape=[
            jax.ShapeDtypeStruct((row_tiles * tile * col_tiles, tile), F32),
            jax.ShapeDtypeStruct((row_tiles * share, tile), F32),
        ],
        scratch_shapes=[
            pltpu.VMEM((feats, col_tiles * tile), BF16),
            pltpu.VMEM((1, col_tiles * tile), F32),
            pltpu.VMEM((col_tiles * tile, 3 * tile), BF16),
            pltpu.VMEM((group * tile, tile), F32),
        ],
        name="schur",
    )(rows, cols, first, noise, inverse)
    return (
        schur.reshape(row_tiles, 1, tile, col_tiles, 1, tile),
        shared.reshape(row_tiles, 1, share, tile),
    )


def solution(mesh):
    placed = (P(None, "prow", None, "pcol"), P(None, "prow", None))
    return jax.shard_map(
        shards,
        mesh=mesh,
        in_specs=placed,
        out_specs=(P(None, "prow", None, None, "pcol", None), P(None, "prow", "pcol", None)),
        check_vma=False,
    )
```

```python
import functools

import jax
import jax.numpy as jnp
from jax import lax
from jax.experimental import pallas as pl
from jax.experimental.pallas import tpu as pltpu
from jax.sharding import PartitionSpec as P

F32 = jnp.float32
BF16 = jnp.bfloat16


def feature_squares(block):
    wide = block.astype(F32)
    return jnp.sum(wide * wide, axis=0, keepdims=True)


def down(row):
    tile = row.shape[1]
    return jnp.transpose(jnp.broadcast_to(row, (tile, tile)))


def eye_mask(tile):
    rows = lax.broadcasted_iota(jnp.int32, (tile, tile), 0)
    cols = lax.broadcasted_iota(jnp.int32, (tile, tile), 1)
    return rows == cols


def split3(panel, left):
    high = panel.astype(BF16)
    low = (panel - high.astype(F32)).astype(BF16)
    return jnp.concatenate([high, high, low] if left else [high, low, high], axis=1)


def matmul(left, right):
    return lax.dot_general(left, right, (((1,), (0,)), ((), ())), preferred_element_type=F32)


def matmul_nt(left, right, precision=None):
    return lax.dot_general(
        left, right, (((1,), (1,)), ((), ())), precision=precision, preferred_element_type=F32
    )


def inverse_factor(first, noise, work):
    feats, tile = first.shape
    sq = feature_squares(first)
    dots = matmul(jnp.transpose(first), first)
    gram = jnp.exp((2.0 * dots - (down(sq) + sq)) * (1.0 / feats))
    diagonal = eye_mask(tile)
    work[...] = gram + jnp.where(diagonal, noise, 0.0)
    part = tile // 4
    for base in range(0, tile, part):
        height = tile - base
        lanes = lax.broadcasted_iota(jnp.int32, (height, tile), 1)
        ids = lax.broadcasted_iota(jnp.int32, (height, tile), 0) + base

        def step(k, carry, base=base, lanes=lanes, ids=ids):
            held = work[base:, :]
            at_k = lanes == k
            pivot = work[pl.ds(k, 1), :]
            here = at_k[:1]
            inv = 1.0 / jnp.sum(jnp.where(here, pivot, 0.0), axis=1, keepdims=True)
            column = jnp.sum(jnp.where(at_k, held, 0.0), axis=1, keepdims=True)
            scaled = jnp.where(here, 1.0, pivot) * inv
            factor = jnp.where(ids > k, column, 0.0)
            cleared = jnp.where(at_k & (ids > k), 0.0, held)
            work[base:, :] = cleared - factor * scaled
            return carry

        lax.fori_loop(base, base + part, step, 0)
    done = work[...]
    pivots = jnp.sum(jnp.where(diagonal, done, 0.0), axis=1, keepdims=True)
    rows = lax.broadcasted_iota(jnp.int32, (tile, tile), 0)
    cols = lax.broadcasted_iota(jnp.int32, (tile, tile), 1)
    unit = jnp.where(cols < rows, done, jnp.where(diagonal, 1.0, 0.0))
    return unit * (1.0 / jnp.sqrt(pivots))


def factor_kernel(first_ref, noise_ref, inverse_ref, work):
    inverse_ref[...] = inverse_factor(
        first_ref[...], noise_ref[...].astype(F32)[:1], work
    )


def schur_kernel(
    row_count, col_count, row_ref, col_ref, first_ref, noise_ref, first_noise_ref, inverse_ref,
    schur_ref, share_ref, wide, col_sq, col_panel, panel, noise_held,
):
    step = pl.program_id(0)
    group, feats, tile = row_ref.shape
    col_tiles = col_ref.shape[0]
    scale = 1.0 / feats
    r, q = lax.axis_index("prow"), lax.axis_index("pcol")
    diagonal = eye_mask(tile)
    first = first_ref[...]
    first_sq = feature_squares(first)
    first_noise = jnp.where(diagonal, first_noise_ref[...].astype(F32)[:1], 0.0)

    def panel_of(samples, sq, leads):
        gram = jnp.exp((2.0 * matmul(samples, first) - (sq + first_sq)) * scale)
        head = gram[:tile] + jnp.where(leads, first_noise, 0.0)
        gram = jnp.concatenate([head, gram[tile:]], axis=0)
        return matmul_nt(gram, inverse_ref[...], lax.Precision.HIGHEST)

    @pl.when(step == 0)
    def _():
        noise_held[...] = noise_ref[...].astype(F32)
        samples, squares = [], []
        for d in range(col_tiles):
            block = col_ref[d]
            place = slice(d * tile, (d + 1) * tile)
            wide[:, place] = block
            sq = feature_squares(block)
            col_sq[:, place] = sq
            samples.append(jnp.transpose(block))
            squares.append(down(sq))
        whole = panel_of(jnp.concatenate(samples), jnp.concatenate(squares), q == 0)
        col_panel[...] = split3(whole, False)

    samples = jnp.concatenate([jnp.transpose(row_ref[t]) for t in range(group)])
    sq = jnp.concatenate([down(feature_squares(row_ref[t])) for t in range(group)])
    rows = panel_of(samples, sq, step * group * row_count + r == 0)
    panel[...] = rows
    dots = matmul(samples, wide[...])
    update = matmul_nt(split3(rows, True), col_panel[...])
    tiles = [step * group + t for t in range(group)]
    noises = [jnp.where(diagonal, noise_held[pl.ds(a, 1), :], 0.0) for a in tiles]
    for d in range(col_tiles):
        place = slice(d * tile, (d + 1) * tile)
        gram = jnp.exp((2.0 * dots[:, place] - (sq + col_sq[:, place])) * scale)
        added = jnp.concatenate([
            jnp.where(a * row_count + r == d * col_count + q, noise, 0.0)
            for a, noise in zip(tiles, noises)
        ])
        schur_ref[pl.ds(d, group * tile, stride=col_tiles), :] = gram + added - update[:, place]
    share = tile // col_count
    share_ref[...] = jnp.concatenate(
        [panel[pl.ds(t * tile + q * share, share), :] for t in range(group)]
    )


def gather_kernel(
    shape, local, noise, rows, cols, first, first_noise,
    held, own_sem, lead_send, lead_recv, x_send, x_recv, z_send, z_recv, y_send, y_recv, root_sem,
):
    nx, nz, ny = shape
    col_tiles, ratio = rows.shape[:2]
    half = col_tiles // 2
    r, q = lax.axis_index("prow"), lax.axis_index("pcol")
    x, z = lax.rem(q, nx), lax.div(q, nx)
    core, y = lax.rem(r, 2), lax.div(r, 2)
    prow, total = 2 * ny, nx * nz
    owner = lax.rem(q, prow)
    side = lax.div(q, prow)
    place = lax.rem(y - lax.div(owner, 2) + ny, ny)
    on_line = core == lax.rem(owner, 2)
    is_root = on_line & (place == 0)
    is_relay = on_line & (place != 0)
    is_lead = r == 0
    far = ny // 2
    away = jnp.minimum(place, ny - place)
    goes_up = place < far
    goes_down = (place == 0) | (place > far + 1)

    def near_z(shift):
        return lax.rem(z + shift + nz, nz)

    def x_peer(k):
        return nx * z + lax.rem(x + k, nx)

    def z_peer(shift):
        return nx * near_z(shift) + x

    def y_peer(shift):
        return 2 * lax.rem(y + shift + ny, ny) + core

    def remote(src, dst, send, recv, row, col):
        return pltpu.make_async_remote_copy(
            src_ref=src, dst_ref=dst, send_sem=send, recv_sem=recv,
            device_id=(row, col), device_id_type=pl.DeviceIdType.MESH,
        )

    barrier = pltpu.get_barrier_semaphore()
    for k in range(1, prow):
        pl.semaphore_signal(
            barrier, device_id=(lax.rem(r + k, prow), q), device_id_type=pl.DeviceIdType.MESH
        )
    peers = [x_peer(k) for k in range(1, nx)] + [z_peer(1), z_peer(-1)]
    for peer in peers:
        pl.semaphore_signal(barrier, device_id=(r, peer), device_id_type=pl.DeviceIdType.MESH)
    pl.semaphore_wait(barrier, prow - 1 + len(peers))

    def lead(k):
        return [
            remote(local.at[0, 0], first.at[z, x], lead_send.at[0, k - 1], lead_recv.at[0], k, q),
            remote(noise, first_noise, lead_send.at[1, k - 1], lead_recv.at[1], k, q),
        ]

    own_lead = [
        pltpu.make_async_copy(local.at[0, 0], first.at[z, x], own_sem.at[1]),
        pltpu.make_async_copy(noise, first_noise, own_sem.at[2]),
    ]

    @pl.when(is_lead)
    def _():
        for k in range(1, prow):
            for copy in lead(k):
                copy.start()
        for copy in own_lead:
            copy.start()

    own = pltpu.make_async_copy(local, rows.at[:, :, z, x], own_sem.at[0])
    own.start()

    def part(chunk, at_z, at_x=None):
        spot = (at_z,) if at_x is None else (at_z, at_x)
        if chunk == 0:
            return first.at[spot]
        tiles = pl.ds((chunk - 1) * half, half)
        return rows.at[(tiles, slice(None), *spot)]

    def x_copy(chunk, k):
        source = part(0, z, x) if chunk == 0 else local.at[pl.ds((chunk - 1) * half, half)]
        return remote(
            source, part(chunk, z, x), x_send.at[chunk, k - 1], x_recv.at[chunk, k - 1], r, x_peer(k)
        )

    for chunk in (1, 2):
        for k in range(1, nx):
            x_copy(chunk, k).start()

    @pl.when(is_lead)
    def _():
        for copy in own_lead:
            copy.wait()

    @pl.when(jnp.logical_not(is_lead))
    def _():
        for copy in lead(1):
            copy.wait_recv()

    for k in range(1, nx):
        x_copy(0, k).start()

    last = nz // 2

    def has(way, step, chunk):
        return step < last or (chunk == 2) == (way == 1)

    def z_send_copy(way, step, chunk):
        toward = 1 if way == 0 else -1
        block = part(chunk, near_z(-toward * (step - 1)))
        return remote(
            block, block, z_send.at[way, step - 1, chunk], z_recv.at[way, step - 1, chunk],
            r, z_peer(toward),
        )

    def z_arrived(way, step, chunk):
        toward = 1 if way == 0 else -1
        block = part(chunk, near_z(-toward * step))
        remote(
            block, block, z_send.at[way, step - 1, chunk], z_recv.at[way, step - 1, chunk],
            r, z_peer(toward),
        ).wait_recv()

    def y_group(step):
        ways = (0,) if step == 0 else (0, 1)
        return [
            (step, way, piece) for piece in (0, 1) for way in ways
            if step == 0 or has(way, step, piece + 1)
        ]

    y_order = [item for step in range(last + 1) for item in y_group(step)]

    def y_place(item):
        step, way, _ = item
        return near_z(-step if way == 0 else step)

    def col_part(item):
        return cols.at[pl.ds(item[2] * half, half), y_place(item)]

    def y_copies(item, from_rows):
        i = y_order.index(item)
        tiles = pl.ds(item[2] * half, half)
        source = rows.at[tiles, side, y_place(item)] if from_rows else col_part(item)
        to = [y_peer(1), y_peer(-1), 2 * y + 1 - core]
        return [
            remote(source, col_part(item), y_send.at[i, n], y_recv.at[i], row, q)
            for n, row in enumerate(to)
        ]

    def each_way(copies, act):
        pl.when(goes_up)(lambda: act(copies[0]))
        pl.when(goes_down)(lambda: act(copies[1]))
        act(copies[2])

    def keep(item):
        i = y_order.index(item)
        tiles = pl.ds(item[2] * half, half)
        buffer = held.at[tiles, y_place(item)]
        return (
            pltpu.make_async_copy(rows.at[tiles, side, y_place(item)], buffer, root_sem.at[0, i]),
            pltpu.make_async_copy(buffer, col_part(item), root_sem.at[1, i]),
        )

    def y_start(item):
        @pl.when(is_root)
        def _():
            each_way(y_copies(item, True), lambda copy: copy.start())
            keep(item)[0].start()

    lags = range(1, far)

    def y_relay(step):
        for lag in lags:
            later = step <= last
            groups = [step - lag] if later else range(max(last + 1 - lag, 0), last + 1)
            groups = [group for group in groups if group >= 0]
            if not groups:
                continue

            @pl.when(is_relay & ((away == lag) if lag != far - 1 else (away >= lag)))
            def _(groups=groups):
                for group in groups:
                    for item in y_group(group):
                        copies = y_copies(item, False)
                        copies[2].wait_recv()
                        each_way(copies, lambda copy: copy.start())

    for chunk in (0, 1, 2):
        if chunk == 1:
            own.wait()
        for k in range(1, nx):
            x_copy(chunk, k).wait_recv()
        for way in (0, 1):
            z_send_copy(way, 1, chunk).start()
        if chunk:
            y_start((0, 0, chunk - 1))
    for step in range(2, last + 2):
        for chunk in (0, 1, 2):
            for way in (0, 1):
                if has(way, step - 1, chunk):
                    z_arrived(way, step - 1, chunk)
                    if step <= last and has(way, step, chunk):
                        z_send_copy(way, step, chunk).start()
                    if chunk:
                        y_start((step - 1, way, chunk - 1))
        y_relay(step - 1)
    y_relay(last + 1)

    @pl.when(is_root)
    def _():
        for item in y_order:
            take, put = keep(item)
            take.wait()
            put.start()
        for item in y_order:
            keep(item)[1].wait()
            each_way(y_copies(item, True), lambda copy: copy.wait_send())

    @pl.when(is_relay)
    def _():
        for item in y_order:
            each_way(y_copies(item, False), lambda copy: copy.wait_send())

    @pl.when(jnp.logical_not(on_line))
    def _():
        for item in y_order:
            y_copies(item, False)[2].wait_recv()

    @pl.when(is_lead)
    def _():
        for k in range(1, prow):
            for copy in lead(k):
                copy.wait_send()

    for chunk in (0, 1, 2):
        for k in range(1, nx):
            x_copy(chunk, k).wait_send()
        for way in (0, 1):
            for step in range(1, last + 1):
                if has(way, step, chunk):
                    z_send_copy(way, step, chunk).wait_send()


def shards(embeddings, noise_var):
    row_count, col_count = lax.axis_size("prow"), lax.axis_size("pcol")
    nx, nz, ny = 4, col_count // 4, row_count // 2
    row_tiles, _, tile, width = embeddings.shape
    ratio = col_count // row_count
    col_tiles = row_tiles // ratio
    local = jnp.transpose(embeddings[:, 0], (0, 2, 1)).reshape(col_tiles, ratio, width, tile)
    pieces = 2 * nz
    anywhere = pl.BlockSpec(memory_space=pl.ANY)
    vmem = pl.BlockSpec(memory_space=pltpu.VMEM)
    dma = pltpu.SemaphoreType.DMA
    rows, cols, first, first_noise = pl.pallas_call(
        functools.partial(gather_kernel, (nx, nz, ny)),
        in_specs=[vmem, vmem],
        out_specs=[anywhere, anywhere, anywhere, vmem],
        out_shape=[
            jax.ShapeDtypeStruct((col_tiles, ratio, nz, nx, width, tile), BF16),
            jax.ShapeDtypeStruct((col_tiles, nz, nx, width, tile), BF16),
            jax.ShapeDtypeStruct((nz, nx, width, tile), BF16),
            jax.ShapeDtypeStruct((row_tiles, tile), BF16),
        ],
        scratch_shapes=[
            pltpu.VMEM((col_tiles, nz, nx, width, tile), BF16),
            dma((3,)),
            dma((2, row_count - 1)),
            dma((2,)),
            dma((3, nx - 1)),
            dma((3, nx - 1)),
            dma((2, nz // 2, 3)),
            dma((2, nz // 2, 3)),
            dma((pieces, 3)),
            dma((pieces,)),
            dma((2, pieces)),
        ],
        compiler_params=pltpu.CompilerParams(collective_id=0, has_side_effects=True),
        name="gather",
    )(local, noise_var[:, 0])
    feats = width * col_count
    return finish(
        rows.reshape(row_tiles, feats, tile),
        cols.reshape(col_tiles, feats, tile),
        first.reshape(feats, tile),
        noise_var,
        first_noise,
    )


def finish(rows, cols, first, noise_var, first_noise):
    row_count, col_count = lax.axis_size("prow"), lax.axis_size("pcol")
    row_tiles, feats, tile = rows.shape
    col_tiles = cols.shape[0]
    noise = noise_var[:, 0]
    inverse = pl.pallas_call(
        factor_kernel,
        out_shape=jax.ShapeDtypeStruct((tile, tile), F32),
        scratch_shapes=[pltpu.VMEM((tile, tile), F32)],
        name="factor",
    )(first, first_noise)
    group = 2
    share = tile // col_count
    height = group * tile * col_tiles
    schur, shared = pl.pallas_call(
        functools.partial(schur_kernel, row_count, col_count),
        grid=(row_tiles // group,),
        in_specs=[
            pl.BlockSpec((group, feats, tile), lambda i: (i, 0, 0)),
            pl.BlockSpec((col_tiles, feats, tile), lambda i: (0, 0, 0)),
            pl.BlockSpec((feats, tile), lambda i: (0, 0)),
            pl.BlockSpec((row_tiles, tile), lambda i: (0, 0)),
            pl.BlockSpec((row_tiles, tile), lambda i: (0, 0)),
            pl.BlockSpec((tile, tile), lambda i: (0, 0)),
        ],
        out_specs=[
            pl.BlockSpec((height, tile), lambda i: (i, 0)),
            pl.BlockSpec((group * share, tile), lambda i: (i, 0)),
        ],
        out_shape=[
            jax.ShapeDtypeStruct((row_tiles * tile * col_tiles, tile), F32),
            jax.ShapeDtypeStruct((row_tiles * share, tile), F32),
        ],
        scratch_shapes=[
            pltpu.VMEM((feats, col_tiles * tile), BF16),
            pltpu.VMEM((1, col_tiles * tile), F32),
            pltpu.VMEM((col_tiles * tile, 3 * tile), BF16),
            pltpu.VMEM((group * tile, tile), F32),
            pltpu.VMEM((row_tiles, tile), F32),
        ],
        name="schur",
    )(rows, cols, first, noise, first_noise, inverse)
    return (
        schur.reshape(row_tiles, 1, tile, col_tiles, 1, tile),
        shared.reshape(row_tiles, 1, share, tile),
    )


def solution(mesh):
    placed = (P(None, "prow", None, "pcol"), P(None, "prow", None))
    return jax.shard_map(
        shards,
        mesh=mesh,
        in_specs=placed,
        out_specs=(P(None, "prow", None, None, "pcol", None), P(None, "prow", "pcol", None)),
        check_vma=False,
    )
```

```python
import functools

import jax
import jax.numpy as jnp
from jax import lax
from jax.experimental import pallas as pl
from jax.experimental.pallas import tpu as pltpu
from jax.sharding import PartitionSpec as P

F32 = jnp.float32
BF16 = jnp.bfloat16


def feature_squares(block):
    wide = block.astype(F32)
    return jnp.sum(wide * wide, axis=0, keepdims=True)


def down(row):
    tile = row.shape[1]
    return jnp.transpose(jnp.broadcast_to(row, (tile, tile)))


def eye_mask(tile):
    rows = lax.broadcasted_iota(jnp.int32, (tile, tile), 0)
    cols = lax.broadcasted_iota(jnp.int32, (tile, tile), 1)
    return rows == cols


def split3(panel, left):
    high = panel.astype(BF16)
    low = (panel - high.astype(F32)).astype(BF16)
    return jnp.concatenate([high, high, low] if left else [high, low, high], axis=1)


def matmul(left, right):
    return lax.dot_general(left, right, (((1,), (0,)), ((), ())), preferred_element_type=F32)


def matmul_nt(left, right, precision=None):
    return lax.dot_general(
        left, right, (((1,), (1,)), ((), ())), precision=precision, preferred_element_type=F32
    )


PIECES = 8


def start_factor(first, noise, work):
    feats = first.shape[0]
    sq = feature_squares(first)
    dots = matmul(jnp.transpose(first), first)
    gram = jnp.exp((2.0 * dots - (down(sq) + sq)) * (1.0 / feats))
    work[...] = gram + jnp.where(eye_mask(first.shape[1]), noise, 0.0)


def eliminate(work, piece):
    tile = work.shape[1]
    part = tile // PIECES
    base = piece * part
    height = tile - base
    lanes = lax.broadcasted_iota(jnp.int32, (height, tile), 1)
    ids = lax.broadcasted_iota(jnp.int32, (height, tile), 0) + base

    def step(k, carry):
        held = work[base:, :]
        at_k = lanes == k
        pivot = work[pl.ds(k, 1), :]
        here = at_k[:1]
        inv = 1.0 / jnp.sum(jnp.where(here, pivot, 0.0), axis=1, keepdims=True)
        column = jnp.sum(jnp.where(at_k, held, 0.0), axis=1, keepdims=True)
        scaled = jnp.where(here, 1.0, pivot) * inv
        factor = jnp.where(ids > k, column, 0.0)
        cleared = jnp.where(at_k & (ids > k), 0.0, held)
        work[base:, :] = cleared - factor * scaled
        return carry

    lax.fori_loop(base, base + part, step, 0)


def end_factor(work):
    tile = work.shape[1]
    diagonal = eye_mask(tile)
    done = work[...]
    pivots = jnp.sum(jnp.where(diagonal, done, 0.0), axis=1, keepdims=True)
    rows = lax.broadcasted_iota(jnp.int32, (tile, tile), 0)
    cols = lax.broadcasted_iota(jnp.int32, (tile, tile), 1)
    unit = jnp.where(cols < rows, done, jnp.where(diagonal, 1.0, 0.0))
    return unit * (1.0 / jnp.sqrt(pivots))


def schur_kernel(
    row_count, col_count, row_ref, col_ref, first_ref, noise_ref, first_noise_ref, inverse_ref,
    schur_ref, share_ref, wide, col_sq, col_panel, panel, noise_held,
):
    step = pl.program_id(0)
    group, feats, tile = row_ref.shape
    col_tiles = col_ref.shape[0]
    scale = 1.0 / feats
    r, q = lax.axis_index("prow"), lax.axis_index("pcol")
    diagonal = eye_mask(tile)
    first = first_ref[...]
    first_sq = feature_squares(first)
    first_noise = jnp.where(diagonal, first_noise_ref[...].astype(F32)[:1], 0.0)

    def panel_of(samples, sq, leads):
        gram = jnp.exp((2.0 * matmul(samples, first) - (sq + first_sq)) * scale)
        head = gram[:tile] + jnp.where(leads, first_noise, 0.0)
        gram = jnp.concatenate([head, gram[tile:]], axis=0)
        return matmul_nt(gram, inverse_ref[...], lax.Precision.HIGHEST)

    @pl.when(step == 0)
    def _():
        noise_held[...] = noise_ref[...].astype(F32)
        samples, squares = [], []
        for d in range(col_tiles):
            block = col_ref[d]
            place = slice(d * tile, (d + 1) * tile)
            wide[:, place] = block
            sq = feature_squares(block)
            col_sq[:, place] = sq
            samples.append(jnp.transpose(block))
            squares.append(down(sq))
        whole = panel_of(jnp.concatenate(samples), jnp.concatenate(squares), q == 0)
        col_panel[...] = split3(whole, False)

    samples = jnp.concatenate([jnp.transpose(row_ref[t]) for t in range(group)])
    sq = jnp.concatenate([down(feature_squares(row_ref[t])) for t in range(group)])
    rows = panel_of(samples, sq, step * group * row_count + r == 0)
    panel[...] = rows
    dots = matmul(samples, wide[...])
    update = matmul_nt(split3(rows, True), col_panel[...])
    tiles = [step * group + t for t in range(group)]
    noises = [jnp.where(diagonal, noise_held[pl.ds(a, 1), :], 0.0) for a in tiles]
    for d in range(col_tiles):
        place = slice(d * tile, (d + 1) * tile)
        gram = jnp.exp((2.0 * dots[:, place] - (sq + col_sq[:, place])) * scale)
        added = jnp.concatenate([
            jnp.where(a * row_count + r == d * col_count + q, noise, 0.0)
            for a, noise in zip(tiles, noises)
        ])
        schur_ref[pl.ds(d, group * tile, stride=col_tiles), :] = gram + added - update[:, place]
    share = tile // col_count
    share_ref[...] = jnp.concatenate(
        [panel[pl.ds(t * tile + q * share, share), :] for t in range(group)]
    )


def gather_kernel(
    shape, local, noise, rows, cols, first, first_noise, inverse,
    held, first_held, work, own_sem, lead_send, lead_recv, x_send, x_recv, z_send, z_recv, y_send, y_recv, root_sem,
):
    nx, nz, ny = shape
    col_tiles, ratio = rows.shape[:2]
    half = col_tiles // 2
    r, q = lax.axis_index("prow"), lax.axis_index("pcol")
    x, z = lax.rem(q, nx), lax.div(q, nx)
    core, y = lax.rem(r, 2), lax.div(r, 2)
    prow, total = 2 * ny, nx * nz
    owner = lax.rem(q, prow)
    side = lax.div(q, prow)
    place = lax.rem(y - lax.div(owner, 2) + ny, ny)
    on_line = core == lax.rem(owner, 2)
    is_root = on_line & (place == 0)
    is_relay = on_line & (place != 0)
    is_lead = r == 0
    far = ny // 2
    away = jnp.minimum(place, ny - place)
    goes_up = place < far
    goes_down = (place == 0) | (place > far + 1)

    def near_z(shift):
        return lax.rem(z + shift + nz, nz)

    def x_peer(k):
        return nx * z + lax.rem(x + k, nx)

    def z_peer(shift):
        return nx * near_z(shift) + x

    def y_peer(shift):
        return 2 * lax.rem(y + shift + ny, ny) + core

    def remote(src, dst, send, recv, row, col):
        return pltpu.make_async_remote_copy(
            src_ref=src, dst_ref=dst, send_sem=send, recv_sem=recv,
            device_id=(row, col), device_id_type=pl.DeviceIdType.MESH,
        )

    barrier = pltpu.get_barrier_semaphore()
    for k in range(1, prow):
        pl.semaphore_signal(
            barrier, device_id=(lax.rem(r + k, prow), q), device_id_type=pl.DeviceIdType.MESH
        )
    peers = [x_peer(k) for k in range(1, nx)] + [z_peer(1), z_peer(-1)]
    for peer in peers:
        pl.semaphore_signal(barrier, device_id=(r, peer), device_id_type=pl.DeviceIdType.MESH)
    pl.semaphore_wait(barrier, prow - 1 + len(peers))

    def lead(k):
        return [
            remote(local.at[0, 0], first.at[z, x], lead_send.at[0, k - 1], lead_recv.at[0], k, q),
            remote(noise, first_noise, lead_send.at[1, k - 1], lead_recv.at[1], k, q),
        ]

    own_lead = [
        pltpu.make_async_copy(local.at[0, 0], first.at[z, x], own_sem.at[1]),
        pltpu.make_async_copy(noise, first_noise, own_sem.at[2]),
    ]

    @pl.when(is_lead)
    def _():
        for k in range(1, prow):
            for copy in lead(k):
                copy.start()
        for copy in own_lead:
            copy.start()

    own = pltpu.make_async_copy(local, rows.at[:, :, z, x], own_sem.at[0])
    own.start()

    def part(chunk, at_z, at_x=None):
        spot = (at_z,) if at_x is None else (at_z, at_x)
        if chunk == 0:
            return first.at[spot]
        tiles = pl.ds((chunk - 1) * half, half)
        return rows.at[(tiles, slice(None), *spot)]

    def x_copy(chunk, k):
        source = part(0, z, x) if chunk == 0 else local.at[pl.ds((chunk - 1) * half, half)]
        return remote(
            source, part(chunk, z, x), x_send.at[chunk, k - 1], x_recv.at[chunk, k - 1], r, x_peer(k)
        )

    for chunk in (1, 2):
        for k in range(1, nx):
            x_copy(chunk, k).start()

    @pl.when(is_lead)
    def _():
        for copy in own_lead:
            copy.wait()

    @pl.when(jnp.logical_not(is_lead))
    def _():
        for copy in lead(1):
            copy.wait_recv()

    for k in range(1, nx):
        x_copy(0, k).start()

    last = nz // 2

    def has(way, step, chunk):
        return step < last or (chunk == 2) == (way == 1)

    def z_send_copy(way, step, chunk):
        toward = 1 if way == 0 else -1
        block = part(chunk, near_z(-toward * (step - 1)))
        return remote(
            block, block, z_send.at[way, step - 1, chunk], z_recv.at[way, step - 1, chunk],
            r, z_peer(toward),
        )

    def z_arrived(way, step, chunk):
        toward = 1 if way == 0 else -1
        block = part(chunk, near_z(-toward * step))
        remote(
            block, block, z_send.at[way, step - 1, chunk], z_recv.at[way, step - 1, chunk],
            r, z_peer(toward),
        ).wait_recv()

    def y_group(step):
        ways = (0,) if step == 0 else (0, 1)
        return [
            (step, way, piece) for piece in (0, 1) for way in ways
            if step == 0 or has(way, step, piece + 1)
        ]

    y_order = [item for step in range(last + 1) for item in y_group(step)]

    def y_place(item):
        step, way, _ = item
        return near_z(-step if way == 0 else step)

    def col_part(item):
        return cols.at[pl.ds(item[2] * half, half), y_place(item)]

    def y_copies(item, from_rows):
        i = y_order.index(item)
        tiles = pl.ds(item[2] * half, half)
        source = rows.at[tiles, side, y_place(item)] if from_rows else col_part(item)
        to = [y_peer(1), y_peer(-1), 2 * y + 1 - core]
        return [
            remote(source, col_part(item), y_send.at[i, n], y_recv.at[i], row, q)
            for n, row in enumerate(to)
        ]

    def each_way(copies, act):
        pl.when(goes_up)(lambda: act(copies[0]))
        pl.when(goes_down)(lambda: act(copies[1]))
        act(copies[2])

    def keep(item):
        i = y_order.index(item)
        tiles = pl.ds(item[2] * half, half)
        buffer = held.at[tiles, y_place(item)]
        return (
            pltpu.make_async_copy(rows.at[tiles, side, y_place(item)], buffer, root_sem.at[0, i]),
            pltpu.make_async_copy(buffer, col_part(item), root_sem.at[1, i]),
        )

    def y_start(item):
        @pl.when(is_root)
        def _():
            each_way(y_copies(item, True), lambda copy: copy.start())
            keep(item)[0].start()

    lags = range(1, far)

    def y_relay(step):
        for lag in lags:
            later = step <= last
            groups = [step - lag] if later else range(max(last + 1 - lag, 0), last + 1)
            groups = [group for group in groups if group >= 0]
            if not groups:
                continue

            @pl.when(is_relay & ((away == lag) if lag != far - 1 else (away >= lag)))
            def _(groups=groups):
                for group in groups:
                    for item in y_group(group):
                        copies = y_copies(item, False)
                        copies[2].wait_recv()
                        each_way(copies, lambda copy: copy.start())

    def z_pass(step, chunk):
        for way in (0, 1):
            if has(way, step, chunk):
                z_arrived(way, step, chunk)
                if step < last and has(way, step + 1, chunk):
                    z_send_copy(way, step + 1, chunk).start()
                if chunk:
                    y_start((step, way, chunk - 1))

    for chunk in (0, 1, 2):
        if chunk == 1:
            own.wait()
        for k in range(1, nx):
            x_copy(chunk, k).wait_recv()
        for way in (0, 1):
            z_send_copy(way, 1, chunk).start()
        if chunk:
            y_start((0, 0, chunk - 1))

    fetch = pltpu.make_async_copy(first, first_held, own_sem.at[3])
    jobs = [functools.partial(eliminate, work, piece) for piece in range(PIECES)]
    ahead = 1
    for step in range(1, last + 1):
        for chunk in (1, 2):
            if ahead <= last:
                z_pass(ahead, 0)
                if ahead == last:
                    fetch.start()
            elif ahead == last + 1:
                fetch.wait()
                leading = first_held[...].astype(F32).reshape(-1, first.shape[-1]).astype(BF16)
                start_factor(leading, first_noise[...].astype(F32)[:1], work)
            else:
                jobs.pop(0)()
            ahead += 1
            z_pass(step, chunk)
        y_relay(step)
    for job in jobs[:2]:
        job()
    y_relay(last + 1)
    for job in jobs[2:]:
        job()
    inverse[...] = end_factor(work)

    @pl.when(is_root)
    def _():
        for item in y_order:
            take, put = keep(item)
            take.wait()
            put.start()
        for item in y_order:
            keep(item)[1].wait()
            each_way(y_copies(item, True), lambda copy: copy.wait_send())

    @pl.when(is_relay)
    def _():
        for item in y_order:
            each_way(y_copies(item, False), lambda copy: copy.wait_send())

    @pl.when(jnp.logical_not(on_line))
    def _():
        for item in y_order:
            y_copies(item, False)[2].wait_recv()

    @pl.when(is_lead)
    def _():
        for k in range(1, prow):
            for copy in lead(k):
                copy.wait_send()

    for chunk in (0, 1, 2):
        for k in range(1, nx):
            x_copy(chunk, k).wait_send()
        for way in (0, 1):
            for step in range(1, last + 1):
                if has(way, step, chunk):
                    z_send_copy(way, step, chunk).wait_send()


def shards(embeddings, noise_var):
    row_count, col_count = lax.axis_size("prow"), lax.axis_size("pcol")
    nx, nz, ny = 4, col_count // 4, row_count // 2
    row_tiles, _, tile, width = embeddings.shape
    ratio = col_count // row_count
    col_tiles = row_tiles // ratio
    local = jnp.transpose(embeddings[:, 0], (0, 2, 1)).reshape(col_tiles, ratio, width, tile)
    pieces = 2 * nz
    anywhere = pl.BlockSpec(memory_space=pl.ANY)
    vmem = pl.BlockSpec(memory_space=pltpu.VMEM)
    dma = pltpu.SemaphoreType.DMA
    rows, cols, first, first_noise, inverse = pl.pallas_call(
        functools.partial(gather_kernel, (nx, nz, ny)),
        in_specs=[vmem, vmem],
        out_specs=[anywhere, anywhere, anywhere, vmem, vmem],
        out_shape=[
            jax.ShapeDtypeStruct((col_tiles, ratio, nz, nx, width, tile), BF16),
            jax.ShapeDtypeStruct((col_tiles, nz, nx, width, tile), BF16),
            jax.ShapeDtypeStruct((nz, nx, width, tile), BF16),
            jax.ShapeDtypeStruct((row_tiles, tile), BF16),
            jax.ShapeDtypeStruct((tile, tile), F32),
        ],
        scratch_shapes=[
            pltpu.VMEM((col_tiles, nz, nx, width, tile), BF16),
            pltpu.VMEM((nz, nx, width, tile), BF16),
            pltpu.VMEM((tile, tile), F32),
            dma((4,)),
            dma((2, row_count - 1)),
            dma((2,)),
            dma((3, nx - 1)),
            dma((3, nx - 1)),
            dma((2, nz // 2, 3)),
            dma((2, nz // 2, 3)),
            dma((pieces, 3)),
            dma((pieces,)),
            dma((2, pieces)),
        ],
        compiler_params=pltpu.CompilerParams(collective_id=0, has_side_effects=True),
        name="gather",
    )(local, noise_var[:, 0])
    feats = width * col_count
    return finish(
        rows.reshape(row_tiles, feats, tile),
        cols.reshape(col_tiles, feats, tile),
        first.reshape(feats, tile),
        noise_var,
        first_noise,
        inverse,
    )


def finish(rows, cols, first, noise_var, first_noise, inverse):
    row_count, col_count = lax.axis_size("prow"), lax.axis_size("pcol")
    row_tiles, feats, tile = rows.shape
    col_tiles = cols.shape[0]
    noise = noise_var[:, 0]
    group = 2
    share = tile // col_count
    height = group * tile * col_tiles
    schur, shared = pl.pallas_call(
        functools.partial(schur_kernel, row_count, col_count),
        grid=(row_tiles // group,),
        in_specs=[
            pl.BlockSpec((group, feats, tile), lambda i: (i, 0, 0)),
            pl.BlockSpec((col_tiles, feats, tile), lambda i: (0, 0, 0)),
            pl.BlockSpec((feats, tile), lambda i: (0, 0)),
            pl.BlockSpec((row_tiles, tile), lambda i: (0, 0)),
            pl.BlockSpec((row_tiles, tile), lambda i: (0, 0)),
            pl.BlockSpec((tile, tile), lambda i: (0, 0)),
        ],
        out_specs=[
            pl.BlockSpec((height, tile), lambda i: (i, 0)),
            pl.BlockSpec((group * share, tile), lambda i: (i, 0)),
        ],
        out_shape=[
            jax.ShapeDtypeStruct((row_tiles * tile * col_tiles, tile), F32),
            jax.ShapeDtypeStruct((row_tiles * share, tile), F32),
        ],
        scratch_shapes=[
            pltpu.VMEM((feats, col_tiles * tile), BF16),
            pltpu.VMEM((1, col_tiles * tile), F32),
            pltpu.VMEM((col_tiles * tile, 3 * tile), BF16),
            pltpu.VMEM((group * tile, tile), F32),
            pltpu.VMEM((row_tiles, tile), F32),
        ],
        name="schur",
    )(rows, cols, first, noise, first_noise, inverse)
    return (
        schur.reshape(row_tiles, 1, tile, col_tiles, 1, tile),
        shared.reshape(row_tiles, 1, share, tile),
    )


def solution(mesh):
    placed = (P(None, "prow", None, "pcol"), P(None, "prow", None))
    return jax.shard_map(
        shards,
        mesh=mesh,
        in_specs=placed,
        out_specs=(P(None, "prow", None, None, "pcol", None), P(None, "prow", "pcol", None)),
        check_vma=False,
    )
```

```python
import functools

import jax
import jax.numpy as jnp
from jax import lax
from jax.experimental import pallas as pl
from jax.experimental.pallas import tpu as pltpu
from jax.sharding import PartitionSpec as P

F32 = jnp.float32
BF16 = jnp.bfloat16


def feature_squares(block):
    wide = block.astype(F32)
    return jnp.sum(wide * wide, axis=0, keepdims=True)


def down(row):
    tile = row.shape[1]
    return jnp.transpose(jnp.broadcast_to(row, (tile, tile)))


def eye_mask(tile):
    rows = lax.broadcasted_iota(jnp.int32, (tile, tile), 0)
    cols = lax.broadcasted_iota(jnp.int32, (tile, tile), 1)
    return rows == cols


def split3(panel, left):
    high = panel.astype(BF16)
    low = (panel - high.astype(F32)).astype(BF16)
    return jnp.concatenate([high, high, low] if left else [high, low, high], axis=1)


def matmul(left, right):
    return lax.dot_general(left, right, (((1,), (0,)), ((), ())), preferred_element_type=F32)


def matmul_nt(left, right, precision=None):
    return lax.dot_general(
        left, right, (((1,), (1,)), ((), ())), precision=precision, preferred_element_type=F32
    )


PIECES = 8


def start_factor(first, noise, work):
    feats = first.shape[0]
    sq = feature_squares(first)
    dots = matmul(jnp.transpose(first), first)
    gram = jnp.exp((2.0 * dots - (down(sq) + sq)) * (1.0 / feats))
    work[...] = gram + jnp.where(eye_mask(first.shape[1]), noise, 0.0)


def eliminate(work, piece):
    tile = work.shape[1]
    part = tile // PIECES
    base = piece * part
    height = tile - base
    lanes = lax.broadcasted_iota(jnp.int32, (height, tile), 1)
    ids = lax.broadcasted_iota(jnp.int32, (height, tile), 0) + base

    def step(k, carry):
        held = work[base:, :]
        at_k = lanes == k
        pivot = work[pl.ds(k, 1), :]
        here = at_k[:1]
        inv = 1.0 / jnp.sum(jnp.where(here, pivot, 0.0), axis=1, keepdims=True)
        column = jnp.sum(jnp.where(at_k, held, 0.0), axis=1, keepdims=True)
        scaled = jnp.where(here, 1.0, pivot) * inv
        factor = jnp.where(ids > k, column, 0.0)
        cleared = jnp.where(at_k & (ids > k), 0.0, held)
        work[base:, :] = cleared - factor * scaled
        return carry

    lax.fori_loop(base, base + part, step, 0)


def end_factor(work):
    tile = work.shape[1]
    diagonal = eye_mask(tile)
    done = work[...]
    pivots = jnp.sum(jnp.where(diagonal, done, 0.0), axis=1, keepdims=True)
    rows = lax.broadcasted_iota(jnp.int32, (tile, tile), 0)
    cols = lax.broadcasted_iota(jnp.int32, (tile, tile), 1)
    unit = jnp.where(cols < rows, done, jnp.where(diagonal, 1.0, 0.0))
    return unit * (1.0 / jnp.sqrt(pivots))


def schur_kernel(
    row_count, col_count, row_ref, col_ref, first_ref, noise_ref, first_noise_ref, inverse_ref,
    schur_ref, share_ref, wide, col_sq, col_panel, panel, noise_held,
):
    step = pl.program_id(0)
    group, feats, tile = row_ref.shape
    col_tiles = col_ref.shape[0]
    scale = 1.0 / feats
    r, q = lax.axis_index("prow"), lax.axis_index("pcol")
    diagonal = eye_mask(tile)
    first = first_ref[...]
    first_sq = feature_squares(first)
    first_noise = jnp.where(diagonal, first_noise_ref[...].astype(F32)[:1], 0.0)

    def panel_of(samples, sq, leads):
        gram = jnp.exp((2.0 * matmul(samples, first) - (sq + first_sq)) * scale)
        head = gram[:tile] + jnp.where(leads, first_noise, 0.0)
        gram = jnp.concatenate([head, gram[tile:]], axis=0)
        return matmul_nt(gram, inverse_ref[...], lax.Precision.HIGHEST)

    @pl.when(step == 0)
    def _():
        noise_held[...] = noise_ref[...].astype(F32)
        samples, squares = [], []
        for d in range(col_tiles):
            block = col_ref[d]
            place = slice(d * tile, (d + 1) * tile)
            wide[:, place] = block
            sq = feature_squares(block)
            col_sq[:, place] = sq
            samples.append(jnp.transpose(block))
            squares.append(down(sq))
        whole = panel_of(jnp.concatenate(samples), jnp.concatenate(squares), q == 0)
        col_panel[...] = split3(whole, False)

    samples = jnp.concatenate([jnp.transpose(row_ref[t]) for t in range(group)])
    sq = jnp.concatenate([down(feature_squares(row_ref[t])) for t in range(group)])
    rows = panel_of(samples, sq, step * group * row_count + r == 0)
    panel[...] = rows
    dots = matmul(samples, wide[...])
    update = matmul_nt(split3(rows, True), col_panel[...])
    tiles = [step * group + t for t in range(group)]
    noises = [jnp.where(diagonal, noise_held[pl.ds(a, 1), :], 0.0) for a in tiles]
    for d in range(col_tiles):
        place = slice(d * tile, (d + 1) * tile)
        gram = jnp.exp((2.0 * dots[:, place] - (sq + col_sq[:, place])) * scale)
        added = jnp.concatenate([
            jnp.where(a * row_count + r == d * col_count + q, noise, 0.0)
            for a, noise in zip(tiles, noises)
        ])
        schur_ref[pl.ds(d, group * tile, stride=col_tiles), :] = gram + added - update[:, place]
    share = tile // col_count
    share_ref[...] = jnp.concatenate(
        [panel[pl.ds(t * tile + q * share, share), :] for t in range(group)]
    )


def gather_kernel(
    shape, local, noise, rows, cols, first, first_noise, inverse,
    held, first_held, work, own_sem, lead_send, lead_recv, x_send, x_recv, z_send, z_recv, y_send, y_recv, root_sem,
):
    nx, nz, ny = shape
    col_tiles, ratio = rows.shape[:2]
    half = col_tiles // 2
    r, q = lax.axis_index("prow"), lax.axis_index("pcol")
    x, z = lax.rem(q, nx), lax.div(q, nx)
    core, y = lax.rem(r, 2), lax.div(r, 2)
    prow, total = 2 * ny, nx * nz
    owner = lax.rem(q, prow)
    side = lax.div(q, prow)
    place = lax.rem(y - lax.div(owner, 2) + ny, ny)
    on_line = core == lax.rem(owner, 2)
    is_root = on_line & (place == 0)
    is_relay = on_line & (place != 0)
    is_lead = r == 0
    far = ny // 2
    away = jnp.minimum(place, ny - place)
    goes_up = place < far
    goes_down = (place == 0) | (place > far + 1)

    def near_z(shift):
        return lax.rem(z + shift + nz, nz)

    def x_peer(k):
        return nx * z + lax.rem(x + k, nx)

    def z_peer(shift):
        return nx * near_z(shift) + x

    def y_peer(shift):
        return 2 * lax.rem(y + shift + ny, ny) + core

    def remote(src, dst, send, recv, row, col):
        return pltpu.make_async_remote_copy(
            src_ref=src, dst_ref=dst, send_sem=send, recv_sem=recv,
            device_id=(row, col), device_id_type=pl.DeviceIdType.MESH,
        )

    barrier = pltpu.get_barrier_semaphore()
    for k in range(1, prow):
        pl.semaphore_signal(
            barrier, device_id=(lax.rem(r + k, prow), q), device_id_type=pl.DeviceIdType.MESH
        )
    peers = [x_peer(k) for k in range(1, nx)] + [z_peer(1), z_peer(-1)]
    for peer in peers:
        pl.semaphore_signal(barrier, device_id=(r, peer), device_id_type=pl.DeviceIdType.MESH)
    pl.semaphore_wait(barrier, prow - 1 + len(peers))

    def lead(k):
        return [
            remote(local.at[0, 0], first.at[z, x], lead_send.at[0, k - 1], lead_recv.at[0], k, q),
            remote(noise, first_noise, lead_send.at[1, k - 1], lead_recv.at[1], k, q),
        ]

    own_lead = [
        pltpu.make_async_copy(local.at[0, 0], first.at[z, x], own_sem.at[1]),
        pltpu.make_async_copy(noise, first_noise, own_sem.at[2]),
    ]

    @pl.when(is_lead)
    def _():
        for k in range(1, prow):
            for copy in lead(k):
                copy.start()
        for copy in own_lead:
            copy.start()

    own = pltpu.make_async_copy(local, rows.at[:, :, z, x], own_sem.at[0])
    own.start()

    def part(chunk, at_z, at_x=None):
        spot = (at_z,) if at_x is None else (at_z, at_x)
        if chunk == 0:
            return first.at[spot]
        tiles = pl.ds((chunk - 1) * half, half)
        return rows.at[(tiles, slice(None), *spot)]

    def x_copy(chunk, k):
        source = part(0, z, x) if chunk == 0 else local.at[pl.ds((chunk - 1) * half, half)]
        return remote(
            source, part(chunk, z, x), x_send.at[chunk, k - 1], x_recv.at[chunk, k - 1], r, x_peer(k)
        )

    for chunk in (1, 2):
        for k in range(1, nx):
            x_copy(chunk, k).start()

    @pl.when(is_lead)
    def _():
        for copy in own_lead:
            copy.wait()

    @pl.when(jnp.logical_not(is_lead))
    def _():
        for copy in lead(1):
            copy.wait_recv()

    for k in range(1, nx):
        x_copy(0, k).start()

    last = nz // 2

    def has(way, step, chunk):
        return step < last or (chunk == 2) == (way == 1)

    def z_send_copy(way, step, chunk):
        toward = 1 if way == 0 else -1
        block = part(chunk, near_z(-toward * (step - 1)))
        return remote(
            block, block, z_send.at[way, step - 1, chunk], z_recv.at[way, step - 1, chunk],
            r, z_peer(toward),
        )

    def z_arrived(way, step, chunk):
        toward = 1 if way == 0 else -1
        block = part(chunk, near_z(-toward * step))
        remote(
            block, block, z_send.at[way, step - 1, chunk], z_recv.at[way, step - 1, chunk],
            r, z_peer(toward),
        ).wait_recv()

    def y_group(step):
        ways = (0,) if step == 0 else (0, 1)
        return [
            (step, way, piece) for piece in (0, 1) for way in ways
            if step == 0 or has(way, step, piece + 1)
        ]

    y_order = [item for step in range(last + 1) for item in y_group(step)]

    def y_place(item):
        step, way, _ = item
        return near_z(-step if way == 0 else step)

    def col_part(item):
        return cols.at[pl.ds(item[2] * half, half), y_place(item)]

    def y_copies(item, from_rows):
        i = y_order.index(item)
        tiles = pl.ds(item[2] * half, half)
        source = rows.at[tiles, side, y_place(item)] if from_rows else col_part(item)
        to = [y_peer(1), y_peer(-1), 2 * y + 1 - core]
        return [
            remote(source, col_part(item), y_send.at[i, n], y_recv.at[i], row, q)
            for n, row in enumerate(to)
        ]

    def each_way(copies, act):
        pl.when(goes_up)(lambda: act(copies[0]))
        pl.when(goes_down)(lambda: act(copies[1]))
        act(copies[2])

    def keep(item):
        i = y_order.index(item)
        tiles = pl.ds(item[2] * half, half)
        buffer = held.at[tiles, y_place(item)]
        return (
            pltpu.make_async_copy(rows.at[tiles, side, y_place(item)], buffer, root_sem.at[0, i]),
            pltpu.make_async_copy(buffer, col_part(item), root_sem.at[1, i]),
        )

    def y_start(item):
        @pl.when(is_root)
        def _():
            each_way(y_copies(item, True), lambda copy: copy.start())
            keep(item)[0].start()

    def event_of(item):
        step, _, piece = item
        return 2 * (step - 1) + piece

    lags = range(1, far)
    events = 2 * last

    def y_relay(now):
        for lag in lags:
            if now < events:
                items = [item for item in y_order if event_of(item) == now - lag]
                if now == 0:
                    items = [item for item in y_order if event_of(item) <= -lag]
            else:
                items = [item for item in y_order if event_of(item) >= events - lag]
            if not items:
                continue

            @pl.when(is_relay & ((away == lag) if lag != far - 1 else (away >= lag)))
            def _(items=items):
                for item in items:
                    copies = y_copies(item, False)
                    copies[2].wait_recv()
                    each_way(copies, lambda copy: copy.start())

    def z_pass(step, chunk):
        for way in (0, 1):
            if has(way, step, chunk):
                z_arrived(way, step, chunk)
                if step < last and has(way, step + 1, chunk):
                    z_send_copy(way, step + 1, chunk).start()
                if chunk:
                    y_start((step, way, chunk - 1))

    for chunk in (0, 1, 2):
        if chunk == 1:
            own.wait()
        if chunk == 2:
            z_pass(1, 0)
        for k in range(1, nx):
            x_copy(chunk, k).wait_recv()
        for way in (0, 1):
            z_send_copy(way, 1, chunk).start()
        if chunk:
            y_start((0, 0, chunk - 1))

    fetch = pltpu.make_async_copy(first, first_held, own_sem.at[3])
    done = 0
    for now in range(events):
        step, chunk = now // 2 + 1, now % 2 + 1
        if now + 2 <= last:
            z_pass(now + 2, 0)
            if now + 2 == last:
                fetch.start()
        elif now + 1 == last:
            fetch.wait()
            leading = first_held[...].astype(F32).reshape(-1, first.shape[-1]).astype(BF16)
            start_factor(leading, first_noise[...].astype(F32)[:1], work)
        else:
            eliminate(work, done)
            done += 1
        z_pass(step, chunk)
        y_relay(now)

    hands_on = is_relay & (away < far)

    def rest():
        for piece in range(done, PIECES):
            eliminate(work, piece)

    pl.when(jnp.logical_not(hands_on))(rest)
    y_relay(events)
    pl.when(hands_on)(rest)
    inverse[...] = end_factor(work)

    @pl.when(is_root)
    def _():
        for item in y_order:
            take, put = keep(item)
            take.wait()
            put.start()
        for item in y_order:
            keep(item)[1].wait()
            each_way(y_copies(item, True), lambda copy: copy.wait_send())

    @pl.when(is_relay)
    def _():
        for item in y_order:
            each_way(y_copies(item, False), lambda copy: copy.wait_send())

    @pl.when(jnp.logical_not(on_line))
    def _():
        for item in y_order:
            y_copies(item, False)[2].wait_recv()

    @pl.when(is_lead)
    def _():
        for k in range(1, prow):
            for copy in lead(k):
                copy.wait_send()

    for chunk in (0, 1, 2):
        for k in range(1, nx):
            x_copy(chunk, k).wait_send()
        for way in (0, 1):
            for step in range(1, last + 1):
                if has(way, step, chunk):
                    z_send_copy(way, step, chunk).wait_send()


def shards(embeddings, noise_var):
    row_count, col_count = lax.axis_size("prow"), lax.axis_size("pcol")
    nx, nz, ny = 4, col_count // 4, row_count // 2
    row_tiles, _, tile, width = embeddings.shape
    ratio = col_count // row_count
    col_tiles = row_tiles // ratio
    local = jnp.transpose(embeddings[:, 0], (0, 2, 1)).reshape(col_tiles, ratio, width, tile)
    pieces = 2 * nz
    anywhere = pl.BlockSpec(memory_space=pl.ANY)
    vmem = pl.BlockSpec(memory_space=pltpu.VMEM)
    dma = pltpu.SemaphoreType.DMA
    rows, cols, first, first_noise, inverse = pl.pallas_call(
        functools.partial(gather_kernel, (nx, nz, ny)),
        in_specs=[vmem, vmem],
        out_specs=[anywhere, anywhere, anywhere, vmem, vmem],
        out_shape=[
            jax.ShapeDtypeStruct((col_tiles, ratio, nz, nx, width, tile), BF16),
            jax.ShapeDtypeStruct((col_tiles, nz, nx, width, tile), BF16),
            jax.ShapeDtypeStruct((nz, nx, width, tile), BF16),
            jax.ShapeDtypeStruct((row_tiles, tile), BF16),
            jax.ShapeDtypeStruct((tile, tile), F32),
        ],
        scratch_shapes=[
            pltpu.VMEM((col_tiles, nz, nx, width, tile), BF16),
            pltpu.VMEM((nz, nx, width, tile), BF16),
            pltpu.VMEM((tile, tile), F32),
            dma((4,)),
            dma((2, row_count - 1)),
            dma((2,)),
            dma((3, nx - 1)),
            dma((3, nx - 1)),
            dma((2, nz // 2, 3)),
            dma((2, nz // 2, 3)),
            dma((pieces, 3)),
            dma((pieces,)),
            dma((2, pieces)),
        ],
        compiler_params=pltpu.CompilerParams(collective_id=0, has_side_effects=True),
        name="gather",
    )(local, noise_var[:, 0])
    feats = width * col_count
    return finish(
        rows.reshape(row_tiles, feats, tile),
        cols.reshape(col_tiles, feats, tile),
        first.reshape(feats, tile),
        noise_var,
        first_noise,
        inverse,
    )


def finish(rows, cols, first, noise_var, first_noise, inverse):
    row_count, col_count = lax.axis_size("prow"), lax.axis_size("pcol")
    row_tiles, feats, tile = rows.shape
    col_tiles = cols.shape[0]
    noise = noise_var[:, 0]
    group = 2
    share = tile // col_count
    height = group * tile * col_tiles
    schur, shared = pl.pallas_call(
        functools.partial(schur_kernel, row_count, col_count),
        grid=(row_tiles // group,),
        in_specs=[
            pl.BlockSpec((group, feats, tile), lambda i: (i, 0, 0)),
            pl.BlockSpec((col_tiles, feats, tile), lambda i: (0, 0, 0)),
            pl.BlockSpec((feats, tile), lambda i: (0, 0)),
            pl.BlockSpec((row_tiles, tile), lambda i: (0, 0)),
            pl.BlockSpec((row_tiles, tile), lambda i: (0, 0)),
            pl.BlockSpec((tile, tile), lambda i: (0, 0)),
        ],
        out_specs=[
            pl.BlockSpec((height, tile), lambda i: (i, 0)),
            pl.BlockSpec((group * share, tile), lambda i: (i, 0)),
        ],
        out_shape=[
            jax.ShapeDtypeStruct((row_tiles * tile * col_tiles, tile), F32),
            jax.ShapeDtypeStruct((row_tiles * share, tile), F32),
        ],
        scratch_shapes=[
            pltpu.VMEM((feats, col_tiles * tile), BF16),
            pltpu.VMEM((1, col_tiles * tile), F32),
            pltpu.VMEM((col_tiles * tile, 3 * tile), BF16),
            pltpu.VMEM((group * tile, tile), F32),
            pltpu.VMEM((row_tiles, tile), F32),
        ],
        name="schur",
    )(rows, cols, first, noise, first_noise, inverse)
    return (
        schur.reshape(row_tiles, 1, tile, col_tiles, 1, tile),
        shared.reshape(row_tiles, 1, share, tile),
    )


def solution(mesh):
    placed = (P(None, "prow", None, "pcol"), P(None, "prow", None))
    return jax.shard_map(
        shards,
        mesh=mesh,
        in_specs=placed,
        out_specs=(P(None, "prow", None, None, "pcol", None), P(None, "prow", "pcol", None)),
        check_vma=False,
    )
```

```python
import functools

import jax
import jax.numpy as jnp
from jax import lax
from jax.experimental import pallas as pl
from jax.experimental.pallas import tpu as pltpu
from jax.sharding import PartitionSpec as P

F32 = jnp.float32
BF16 = jnp.bfloat16


def feature_squares(block):
    wide = block.astype(F32)
    return jnp.sum(wide * wide, axis=0, keepdims=True)


def down(row):
    tile = row.shape[1]
    return jnp.transpose(jnp.broadcast_to(row, (tile, tile)))


def eye_mask(tile):
    rows = lax.broadcasted_iota(jnp.int32, (tile, tile), 0)
    cols = lax.broadcasted_iota(jnp.int32, (tile, tile), 1)
    return rows == cols


def split3(panel, left):
    high = panel.astype(BF16)
    low = (panel - high.astype(F32)).astype(BF16)
    return jnp.concatenate([high, high, low] if left else [high, low, high], axis=1)


def matmul(left, right):
    return lax.dot_general(left, right, (((1,), (0,)), ((), ())), preferred_element_type=F32)


def matmul_nt(left, right, precision=None):
    return lax.dot_general(
        left, right, (((1,), (1,)), ((), ())), precision=precision, preferred_element_type=F32
    )


PIECES = 8


def start_factor(first, noise, work):
    feats = first.shape[0]
    sq = feature_squares(first)
    dots = matmul(jnp.transpose(first), first)
    gram = jnp.exp((2.0 * dots - (down(sq) + sq)) * (1.0 / feats))
    work[...] = gram + jnp.where(eye_mask(first.shape[1]), noise, 0.0)


def eliminate(work, piece):
    tile = work.shape[1]
    part = tile // PIECES
    base = piece * part
    height = tile - base
    lanes = lax.broadcasted_iota(jnp.int32, (height, tile), 1)
    ids = lax.broadcasted_iota(jnp.int32, (height, tile), 0) + base

    def step(k, carry):
        held = work[base:, :]
        at_k = lanes == k
        pivot = work[pl.ds(k, 1), :]
        here = at_k[:1]
        inv = 1.0 / jnp.sum(jnp.where(here, pivot, 0.0), axis=1, keepdims=True)
        column = jnp.sum(jnp.where(at_k, held, 0.0), axis=1, keepdims=True)
        scaled = jnp.where(here, 1.0, pivot) * inv
        factor = jnp.where(ids > k, column, 0.0)
        cleared = jnp.where(at_k & (ids > k), 0.0, held)
        work[base:, :] = cleared - factor * scaled
        return carry

    lax.fori_loop(base, base + part, step, 0)


def end_factor(work):
    tile = work.shape[1]
    diagonal = eye_mask(tile)
    done = work[...]
    pivots = jnp.sum(jnp.where(diagonal, done, 0.0), axis=1, keepdims=True)
    rows = lax.broadcasted_iota(jnp.int32, (tile, tile), 0)
    cols = lax.broadcasted_iota(jnp.int32, (tile, tile), 1)
    unit = jnp.where(cols < rows, done, jnp.where(diagonal, 1.0, 0.0))
    return unit * (1.0 / jnp.sqrt(pivots))


def schur_kernel(
    row_count, col_count, row_ref, col_ref, first_ref, noise_ref, first_noise_ref, inverse_ref,
    schur_ref, share_ref, wide, col_sq, col_panel, panel, noise_held,
):
    step = pl.program_id(0)
    group, feats, tile = row_ref.shape
    col_tiles = col_ref.shape[0]
    scale = 1.0 / feats
    r, q = lax.axis_index("prow"), lax.axis_index("pcol")
    diagonal = eye_mask(tile)
    first = first_ref[...]
    first_sq = feature_squares(first)
    first_noise = jnp.where(diagonal, first_noise_ref[...].astype(F32)[:1], 0.0)

    def panel_of(samples, sq, leads):
        gram = jnp.exp((2.0 * matmul(samples, first) - (sq + first_sq)) * scale)
        head = gram[:tile] + jnp.where(leads, first_noise, 0.0)
        gram = jnp.concatenate([head, gram[tile:]], axis=0)
        return matmul_nt(gram, inverse_ref[...], lax.Precision.HIGHEST)

    @pl.when(step == 0)
    def _():
        noise_held[...] = noise_ref[...].astype(F32)
        samples, squares = [], []
        for d in range(col_tiles):
            block = col_ref[d]
            place = slice(d * tile, (d + 1) * tile)
            wide[:, place] = block
            sq = feature_squares(block)
            col_sq[:, place] = sq
            samples.append(jnp.transpose(block))
            squares.append(down(sq))
        whole = panel_of(jnp.concatenate(samples), jnp.concatenate(squares), q == 0)
        col_panel[...] = split3(whole, False)

    samples = jnp.concatenate([jnp.transpose(row_ref[t]) for t in range(group)])
    sq = jnp.concatenate([down(feature_squares(row_ref[t])) for t in range(group)])
    rows = panel_of(samples, sq, step * group * row_count + r == 0)
    panel[...] = rows
    dots = matmul(samples, wide[...])
    update = matmul_nt(split3(rows, True), col_panel[...])
    tiles = [step * group + t for t in range(group)]
    noises = [jnp.where(diagonal, noise_held[pl.ds(a, 1), :], 0.0) for a in tiles]
    for d in range(col_tiles):
        place = slice(d * tile, (d + 1) * tile)
        gram = jnp.exp((2.0 * dots[:, place] - (sq + col_sq[:, place])) * scale)
        added = jnp.concatenate([
            jnp.where(a * row_count + r == d * col_count + q, noise, 0.0)
            for a, noise in zip(tiles, noises)
        ])
        schur_ref[pl.ds(d, group * tile, stride=col_tiles), :] = gram + added - update[:, place]
    share = tile // col_count
    share_ref[...] = jnp.concatenate(
        [panel[pl.ds(t * tile + q * share, share), :] for t in range(group)]
    )


def gather_kernel(
    shape, local, noise, rows, cols, first, first_noise, inverse,
    held, first_held, work, own_sem, lead_send, lead_recv, x_send, x_recv, z_send, z_recv, y_send, y_recv, root_sem, share_sem,
):
    nx, nz, ny = shape
    col_tiles, ratio = rows.shape[:2]
    half = col_tiles // 2
    r, q = lax.axis_index("prow"), lax.axis_index("pcol")
    x, z = lax.rem(q, nx), lax.div(q, nx)
    core, y = lax.rem(r, 2), lax.div(r, 2)
    prow, total = 2 * ny, nx * nz
    owner = lax.rem(q, prow)
    side = lax.div(q, prow)
    place = lax.rem(y - lax.div(owner, 2) + ny, ny)
    on_line = core == lax.rem(owner, 2)
    is_root = on_line & (place == 0)
    is_relay = on_line & (place != 0)
    is_lead = r == 0
    far = ny // 2
    away = jnp.minimum(place, ny - place)
    goes_up = place < far
    goes_down = (place == 0) | (place > far + 1)

    def near_z(shift):
        return lax.rem(z + shift + nz, nz)

    def x_peer(k):
        return nx * z + lax.rem(x + k, nx)

    def z_peer(shift):
        return nx * near_z(shift) + x

    def y_peer(shift):
        return 2 * lax.rem(y + shift + ny, ny) + core

    def remote(src, dst, send, recv, row, col):
        return pltpu.make_async_remote_copy(
            src_ref=src, dst_ref=dst, send_sem=send, recv_sem=recv,
            device_id=(row, col), device_id_type=pl.DeviceIdType.MESH,
        )

    barrier = pltpu.get_barrier_semaphore()
    for k in range(1, prow):
        pl.semaphore_signal(
            barrier, device_id=(lax.rem(r + k, prow), q), device_id_type=pl.DeviceIdType.MESH
        )
    peers = [x_peer(k) for k in range(1, nx)] + [z_peer(1), z_peer(-1)]
    for peer in peers:
        pl.semaphore_signal(barrier, device_id=(r, peer), device_id_type=pl.DeviceIdType.MESH)
    pl.semaphore_wait(barrier, prow - 1 + len(peers))

    def lead(k):
        return [
            remote(local.at[0, 0], first.at[z, x], lead_send.at[0, k - 1], lead_recv.at[0], k, q),
            remote(noise, first_noise, lead_send.at[1, k - 1], lead_recv.at[1], k, q),
        ]

    own_lead = [
        pltpu.make_async_copy(local.at[0, 0], first.at[z, x], own_sem.at[1]),
        pltpu.make_async_copy(noise, first_noise, own_sem.at[2]),
    ]

    @pl.when(is_lead)
    def _():
        for k in range(1, prow):
            for copy in lead(k):
                copy.start()
        for copy in own_lead:
            copy.start()

    own = pltpu.make_async_copy(local, rows.at[:, :, z, x], own_sem.at[0])
    own.start()

    def part(chunk, at_z, at_x=None):
        spot = (at_z,) if at_x is None else (at_z, at_x)
        if chunk == 0:
            return first.at[spot]
        tiles = pl.ds((chunk - 1) * half, half)
        return rows.at[(tiles, slice(None), *spot)]

    def x_copy(chunk, k):
        source = part(0, z, x) if chunk == 0 else local.at[pl.ds((chunk - 1) * half, half)]
        return remote(
            source, part(chunk, z, x), x_send.at[chunk, k - 1], x_recv.at[chunk, k - 1], r, x_peer(k)
        )

    for chunk in (1, 2):
        for k in range(1, nx):
            x_copy(chunk, k).start()

    @pl.when(is_lead)
    def _():
        for copy in own_lead:
            copy.wait()

    @pl.when(jnp.logical_not(is_lead))
    def _():
        for copy in lead(1):
            copy.wait_recv()

    for k in range(1, nx):
        x_copy(0, k).start()

    last = nz // 2

    def has(way, step, chunk):
        return step < last or (chunk == 2) == (way == 1)

    def z_send_copy(way, step, chunk):
        toward = 1 if way == 0 else -1
        block = part(chunk, near_z(-toward * (step - 1)))
        return remote(
            block, block, z_send.at[way, step - 1, chunk], z_recv.at[way, step - 1, chunk],
            r, z_peer(toward),
        )

    def z_arrived(way, step, chunk):
        toward = 1 if way == 0 else -1
        block = part(chunk, near_z(-toward * step))
        remote(
            block, block, z_send.at[way, step - 1, chunk], z_recv.at[way, step - 1, chunk],
            r, z_peer(toward),
        ).wait_recv()

    def y_group(step):
        ways = (0,) if step == 0 else (0, 1)
        return [
            (step, way, piece) for piece in (0, 1) for way in ways
            if step == 0 or has(way, step, piece + 1)
        ]

    y_order = [item for step in range(last + 1) for item in y_group(step)]

    def y_place(item):
        step, way, _ = item
        return near_z(-step if way == 0 else step)

    def col_part(item):
        return cols.at[pl.ds(item[2] * half, half), y_place(item)]

    def y_copies(item, from_rows):
        i = y_order.index(item)
        tiles = pl.ds(item[2] * half, half)
        source = rows.at[tiles, side, y_place(item)] if from_rows else col_part(item)
        to = [y_peer(1), y_peer(-1), 2 * y + 1 - core]
        return [
            remote(source, col_part(item), y_send.at[i, n], y_recv.at[i], row, q)
            for n, row in enumerate(to)
        ]

    def each_way(copies, act):
        pl.when(goes_up)(lambda: act(copies[0]))
        pl.when(goes_down)(lambda: act(copies[1]))
        act(copies[2])

    def keep(item):
        i = y_order.index(item)
        tiles = pl.ds(item[2] * half, half)
        buffer = held.at[tiles, y_place(item)]
        return (
            pltpu.make_async_copy(rows.at[tiles, side, y_place(item)], buffer, root_sem.at[0, i]),
            pltpu.make_async_copy(buffer, col_part(item), root_sem.at[1, i]),
        )

    def y_start(item):
        @pl.when(is_root)
        def _():
            each_way(y_copies(item, True), lambda copy: copy.start())
            keep(item)[0].start()

    def event_of(item):
        step, _, piece = item
        return 2 * (step - 1) + piece

    lags = range(1, far)
    events = 2 * last

    def y_relay(now):
        for lag in lags:
            if now < events:
                items = [item for item in y_order if event_of(item) == now - lag]
                if now == 0:
                    items = [item for item in y_order if event_of(item) <= -lag]
            else:
                items = [item for item in y_order if event_of(item) >= events - lag]
            if not items:
                continue

            @pl.when(is_relay & ((away == lag) if lag != far - 1 else (away >= lag)))
            def _(items=items):
                for item in items:
                    copies = y_copies(item, False)
                    copies[2].wait_recv()
                    each_way(copies, lambda copy: copy.start())

    def z_pass(step, chunk):
        for way in (0, 1):
            if has(way, step, chunk):
                z_arrived(way, step, chunk)
                if step < last and has(way, step + 1, chunk):
                    z_send_copy(way, step + 1, chunk).start()
                if chunk:
                    y_start((step, way, chunk - 1))

    for chunk in (0, 1, 2):
        if chunk == 1:
            own.wait()
        if chunk == 2:
            z_pass(1, 0)
        for k in range(1, nx):
            x_copy(chunk, k).wait_recv()
        for way in (0, 1):
            z_send_copy(way, 1, chunk).start()
        if chunk:
            y_start((0, 0, chunk - 1))

    fetch = pltpu.make_async_copy(first, first_held, own_sem.at[3])
    off_line = jnp.logical_not(on_line)

    def begin():
        fetch.wait()
        leading = first_held[...].astype(F32).reshape(-1, first.shape[-1]).astype(BF16)
        start_factor(leading, first_noise[...].astype(F32)[:1], work)

    done = 0
    for now in range(events):
        step, chunk = now // 2 + 1, now % 2 + 1
        if now + 2 <= last:
            z_pass(now + 2, 0)
            if now + 2 == last:
                pl.when(off_line)(fetch.start)
        elif now + 1 == last:
            pl.when(off_line)(begin)
        else:
            pl.when(off_line)(functools.partial(eliminate, work, done))
            done += 1
        z_pass(step, chunk)
        y_relay(now)

    @pl.when(off_line)
    def _():
        for piece in range(done, PIECES):
            eliminate(work, piece)
        inverse[...] = end_factor(work)

    y_relay(events)
    handed = remote(inverse, inverse, share_sem.at[0], share_sem.at[1], 2 * y + 1 - core, q)

    @pl.when(is_root)
    def _():
        for item in y_order:
            take, put = keep(item)
            take.wait()
            put.start()
        for item in y_order:
            keep(item)[1].wait()
            each_way(y_copies(item, True), lambda copy: copy.wait_send())

    @pl.when(is_relay)
    def _():
        for item in y_order:
            each_way(y_copies(item, False), lambda copy: copy.wait_send())

    @pl.when(off_line)
    def _():
        late = [item for item in y_order if event_of(item) >= events - far]
        for item in y_order:
            if item not in late:
                y_copies(item, False)[2].wait_recv()
        handed.start()
        for item in late:
            y_copies(item, False)[2].wait_recv()
        handed.wait_send()

    pl.when(on_line)(handed.wait_recv)

    @pl.when(is_lead)
    def _():
        for k in range(1, prow):
            for copy in lead(k):
                copy.wait_send()

    for chunk in (0, 1, 2):
        for k in range(1, nx):
            x_copy(chunk, k).wait_send()
        for way in (0, 1):
            for step in range(1, last + 1):
                if has(way, step, chunk):
                    z_send_copy(way, step, chunk).wait_send()


def shards(embeddings, noise_var):
    row_count, col_count = lax.axis_size("prow"), lax.axis_size("pcol")
    nx, nz, ny = 4, col_count // 4, row_count // 2
    row_tiles, _, tile, width = embeddings.shape
    ratio = col_count // row_count
    col_tiles = row_tiles // ratio
    local = jnp.transpose(embeddings[:, 0], (0, 2, 1)).reshape(col_tiles, ratio, width, tile)
    pieces = 2 * nz
    anywhere = pl.BlockSpec(memory_space=pl.ANY)
    vmem = pl.BlockSpec(memory_space=pltpu.VMEM)
    dma = pltpu.SemaphoreType.DMA
    rows, cols, first, first_noise, inverse = pl.pallas_call(
        functools.partial(gather_kernel, (nx, nz, ny)),
        in_specs=[vmem, vmem],
        out_specs=[anywhere, anywhere, anywhere, vmem, vmem],
        out_shape=[
            jax.ShapeDtypeStruct((col_tiles, ratio, nz, nx, width, tile), BF16),
            jax.ShapeDtypeStruct((col_tiles, nz, nx, width, tile), BF16),
            jax.ShapeDtypeStruct((nz, nx, width, tile), BF16),
            jax.ShapeDtypeStruct((row_tiles, tile), BF16),
            jax.ShapeDtypeStruct((tile, tile), F32),
        ],
        scratch_shapes=[
            pltpu.VMEM((col_tiles, nz, nx, width, tile), BF16),
            pltpu.VMEM((nz, nx, width, tile), BF16),
            pltpu.VMEM((tile, tile), F32),
            dma((4,)),
            dma((2, row_count - 1)),
            dma((2,)),
            dma((3, nx - 1)),
            dma((3, nx - 1)),
            dma((2, nz // 2, 3)),
            dma((2, nz // 2, 3)),
            dma((pieces, 3)),
            dma((pieces,)),
            dma((2, pieces)),
            dma((2,)),
        ],
        compiler_params=pltpu.CompilerParams(collective_id=0, has_side_effects=True),
        name="gather",
    )(local, noise_var[:, 0])
    feats = width * col_count
    return finish(
        rows.reshape(row_tiles, feats, tile),
        cols.reshape(col_tiles, feats, tile),
        first.reshape(feats, tile),
        noise_var,
        first_noise,
        inverse,
    )


def finish(rows, cols, first, noise_var, first_noise, inverse):
    row_count, col_count = lax.axis_size("prow"), lax.axis_size("pcol")
    row_tiles, feats, tile = rows.shape
    col_tiles = cols.shape[0]
    noise = noise_var[:, 0]
    group = 2
    share = tile // col_count
    height = group * tile * col_tiles
    schur, shared = pl.pallas_call(
        functools.partial(schur_kernel, row_count, col_count),
        grid=(row_tiles // group,),
        in_specs=[
            pl.BlockSpec((group, feats, tile), lambda i: (i, 0, 0)),
            pl.BlockSpec((col_tiles, feats, tile), lambda i: (0, 0, 0)),
            pl.BlockSpec((feats, tile), lambda i: (0, 0)),
            pl.BlockSpec((row_tiles, tile), lambda i: (0, 0)),
            pl.BlockSpec((row_tiles, tile), lambda i: (0, 0)),
            pl.BlockSpec((tile, tile), lambda i: (0, 0)),
        ],
        out_specs=[
            pl.BlockSpec((height, tile), lambda i: (i, 0)),
            pl.BlockSpec((group * share, tile), lambda i: (i, 0)),
        ],
        out_shape=[
            jax.ShapeDtypeStruct((row_tiles * tile * col_tiles, tile), F32),
            jax.ShapeDtypeStruct((row_tiles * share, tile), F32),
        ],
        scratch_shapes=[
            pltpu.VMEM((feats, col_tiles * tile), BF16),
            pltpu.VMEM((1, col_tiles * tile), F32),
            pltpu.VMEM((col_tiles * tile, 3 * tile), BF16),
            pltpu.VMEM((group * tile, tile), F32),
            pltpu.VMEM((row_tiles, tile), F32),
        ],
        name="schur",
    )(rows, cols, first, noise, first_noise, inverse)
    return (
        schur.reshape(row_tiles, 1, tile, col_tiles, 1, tile),
        shared.reshape(row_tiles, 1, share, tile),
    )


def solution(mesh):
    placed = (P(None, "prow", None, "pcol"), P(None, "prow", None))
    return jax.shard_map(
        shards,
        mesh=mesh,
        in_specs=placed,
        out_specs=(P(None, "prow", None, None, "pcol", None), P(None, "prow", "pcol", None)),
        check_vma=False,
    )
```

```python
import functools

import jax
import jax.numpy as jnp
from jax import lax
from jax.experimental import pallas as pl
from jax.experimental.pallas import tpu as pltpu
from jax.sharding import PartitionSpec as P

F32 = jnp.float32
BF16 = jnp.bfloat16


def feature_squares(block):
    wide = block.astype(F32)
    return jnp.sum(wide * wide, axis=0, keepdims=True)


def down(row):
    tile = row.shape[1]
    return jnp.transpose(jnp.broadcast_to(row, (tile, tile)))


def eye_mask(tile):
    rows = lax.broadcasted_iota(jnp.int32, (tile, tile), 0)
    cols = lax.broadcasted_iota(jnp.int32, (tile, tile), 1)
    return rows == cols


def split3(panel, left):
    high = panel.astype(BF16)
    low = (panel - high.astype(F32)).astype(BF16)
    return jnp.concatenate([high, high, low] if left else [high, low, high], axis=1)


def matmul(left, right):
    return lax.dot_general(left, right, (((1,), (0,)), ((), ())), preferred_element_type=F32)


def matmul_nt(left, right, precision=None):
    return lax.dot_general(
        left, right, (((1,), (1,)), ((), ())), precision=precision, preferred_element_type=F32
    )


PIECES = 8


def start_factor(first, noise, work):
    feats = first.shape[0]
    sq = feature_squares(first)
    dots = matmul(jnp.transpose(first), first)
    gram = jnp.exp((2.0 * dots - (down(sq) + sq)) * (1.0 / feats))
    work[...] = gram + jnp.where(eye_mask(first.shape[1]), noise, 0.0)


def eliminate(work, piece):
    tile = work.shape[1]
    part = tile // PIECES
    base = piece * part
    height = tile - base
    lanes = lax.broadcasted_iota(jnp.int32, (height, tile), 1)
    ids = lax.broadcasted_iota(jnp.int32, (height, tile), 0) + base

    def step(k, carry):
        held = work[base:, :]
        at_k = lanes == k
        pivot = work[pl.ds(k, 1), :]
        here = at_k[:1]
        inv = 1.0 / jnp.sum(jnp.where(here, pivot, 0.0), axis=1, keepdims=True)
        column = jnp.sum(jnp.where(at_k, held, 0.0), axis=1, keepdims=True)
        scaled = jnp.where(here, 1.0, pivot) * inv
        factor = jnp.where(ids > k, column, 0.0)
        cleared = jnp.where(at_k & (ids > k), 0.0, held)
        work[base:, :] = cleared - factor * scaled
        return carry

    lax.fori_loop(base, base + part, step, 0)


def end_factor(work):
    tile = work.shape[1]
    diagonal = eye_mask(tile)
    done = work[...]
    pivots = jnp.sum(jnp.where(diagonal, done, 0.0), axis=1, keepdims=True)
    rows = lax.broadcasted_iota(jnp.int32, (tile, tile), 0)
    cols = lax.broadcasted_iota(jnp.int32, (tile, tile), 1)
    unit = jnp.where(cols < rows, done, jnp.where(diagonal, 1.0, 0.0))
    return unit * (1.0 / jnp.sqrt(pivots))


def schur_kernel(
    row_count, col_count, row_ref, col_ref, first_ref, noise_ref, first_noise_ref, inverse_ref,
    schur_ref, share_ref, wide, col_sq, col_panel, panel, noise_held,
):
    step = pl.program_id(0)
    group, feats, tile = row_ref.shape
    col_tiles = col_ref.shape[0]
    scale = 1.0 / feats
    r, q = lax.axis_index("prow"), lax.axis_index("pcol")
    diagonal = eye_mask(tile)
    first = first_ref[...]
    first_sq = feature_squares(first)
    first_noise = jnp.where(diagonal, first_noise_ref[...].astype(F32)[:1], 0.0)

    def panel_of(samples, sq, leads):
        gram = jnp.exp((2.0 * matmul(samples, first) - (sq + first_sq)) * scale)
        head = gram[:tile] + jnp.where(leads, first_noise, 0.0)
        gram = jnp.concatenate([head, gram[tile:]], axis=0)
        return matmul_nt(gram, inverse_ref[...], lax.Precision.HIGHEST)

    @pl.when(step == 0)
    def _():
        noise_held[...] = noise_ref[...].astype(F32)
        samples, squares = [], []
        for d in range(col_tiles):
            block = col_ref[d]
            place = slice(d * tile, (d + 1) * tile)
            wide[:, place] = block
            sq = feature_squares(block)
            col_sq[:, place] = sq
            samples.append(jnp.transpose(block))
            squares.append(down(sq))
        whole = panel_of(jnp.concatenate(samples), jnp.concatenate(squares), q == 0)
        col_panel[...] = split3(whole, False)

    samples = jnp.concatenate([jnp.transpose(row_ref[t]) for t in range(group)])
    sq = jnp.concatenate([down(feature_squares(row_ref[t])) for t in range(group)])
    rows = panel_of(samples, sq, step * group * row_count + r == 0)
    panel[...] = rows
    dots = matmul(samples, wide[...])
    update = matmul_nt(split3(rows, True), col_panel[...])
    tiles = [step * group + t for t in range(group)]
    noises = [jnp.where(diagonal, noise_held[pl.ds(a, 1), :], 0.0) for a in tiles]
    for d in range(col_tiles):
        place = slice(d * tile, (d + 1) * tile)
        gram = jnp.exp((2.0 * dots[:, place] - (sq + col_sq[:, place])) * scale)
        added = jnp.concatenate([
            jnp.where(a * row_count + r == d * col_count + q, noise, 0.0)
            for a, noise in zip(tiles, noises)
        ])
        schur_ref[pl.ds(d, group * tile, stride=col_tiles), :] = gram + added - update[:, place]
    share = tile // col_count
    share_ref[...] = jnp.concatenate(
        [panel[pl.ds(t * tile + q * share, share), :] for t in range(group)]
    )


def gather_kernel(
    shape, local, noise, rows, cols, first, first_noise, inverse,
    held, first_held, work, own_sem, lead_send, lead_recv, x_send, x_recv, z_send, z_recv, y_send, y_recv, root_sem, share_sem,
):
    nx, nz, ny = shape
    col_tiles, ratio = rows.shape[:2]
    half = col_tiles // 2
    r, q = lax.axis_index("prow"), lax.axis_index("pcol")
    x, z = lax.rem(q, nx), lax.div(q, nx)
    core, y = lax.rem(r, 2), lax.div(r, 2)
    prow, total = 2 * ny, nx * nz
    owner = lax.rem(q, prow)
    side = lax.div(q, prow)
    place = lax.rem(y - lax.div(owner, 2) + ny, ny)
    main = core == lax.rem(owner, 2)
    relay_core = 1 - lax.rem(owner, 2)
    is_root = main & (place == 0)
    is_relay = jnp.logical_not(main) & (place != 0)
    is_end = jnp.logical_not(is_root | is_relay)
    owner_ring = lax.rem(r, nx) == x
    is_lead = r == 0
    far = ny // 2
    away = jnp.minimum(place, ny - place)
    goes_up = place < far
    goes_down = (place == 0) | (place > far + 1)

    def near_z(shift):
        return lax.rem(z + shift + nz, nz)

    def x_peer(k):
        return nx * z + lax.rem(x + k, nx)

    def z_peer(shift):
        return nx * near_z(shift) + x

    def y_peer(shift):
        return 2 * lax.rem(y + shift + ny, ny) + relay_core

    def remote(src, dst, send, recv, row, col):
        return pltpu.make_async_remote_copy(
            src_ref=src, dst_ref=dst, send_sem=send, recv_sem=recv,
            device_id=(row, col), device_id_type=pl.DeviceIdType.MESH,
        )

    barrier = pltpu.get_barrier_semaphore()
    for k in range(1, prow):
        pl.semaphore_signal(
            barrier, device_id=(lax.rem(r + k, prow), q), device_id_type=pl.DeviceIdType.MESH
        )
    peers = [x_peer(k) for k in range(1, nx)] + [z_peer(1), z_peer(-1)]
    for peer in peers:
        pl.semaphore_signal(barrier, device_id=(r, peer), device_id_type=pl.DeviceIdType.MESH)
    pl.semaphore_wait(barrier, prow - 1 + len(peers))

    def lead(k):
        return [
            remote(local.at[0, 0], first.at[z, x], lead_send.at[0, k - 1], lead_recv.at[0], k, q),
            remote(noise, first_noise, lead_send.at[1, k - 1], lead_recv.at[1], k, q),
        ]

    own_lead = [
        pltpu.make_async_copy(local.at[0, 0], first.at[z, x], own_sem.at[1]),
        pltpu.make_async_copy(noise, first_noise, own_sem.at[2]),
    ]

    @pl.when(is_lead)
    def _():
        for k in range(1, prow):
            for copy in lead(k):
                copy.start()
        for copy in own_lead:
            copy.start()

    own = pltpu.make_async_copy(local, rows.at[:, :, z, x], own_sem.at[0])
    own.start()

    def part(chunk, at_z, at_x=None):
        spot = (at_z,) if at_x is None else (at_z, at_x)
        if chunk == 0:
            return first.at[spot]
        tiles = pl.ds((chunk - 1) * half, half)
        return rows.at[(tiles, slice(None), *spot)]

    def x_copy(chunk, k):
        source = part(0, z, x) if chunk == 0 else local.at[pl.ds((chunk - 1) * half, half)]
        return remote(
            source, part(chunk, z, x), x_send.at[chunk, k - 1], x_recv.at[chunk, k - 1], r, x_peer(k)
        )

    for chunk in (1, 2):
        for k in range(1, nx):
            x_copy(chunk, k).start()

    @pl.when(is_lead)
    def _():
        for copy in own_lead:
            copy.wait()

    @pl.when(jnp.logical_not(is_lead))
    def _():
        for copy in lead(1):
            copy.wait_recv()

    for k in range(1, nx):
        x_copy(0, k).start()

    last = nz // 2

    def has(way, step, chunk):
        return step < last or (chunk == 2) == (way == 1)

    def z_send_copy(way, step, chunk):
        toward = 1 if way == 0 else -1
        block = part(chunk, near_z(-toward * (step - 1)))
        return remote(
            block, block, z_send.at[way, step - 1, chunk], z_recv.at[way, step - 1, chunk],
            r, z_peer(toward),
        )

    def z_arrived(way, step, chunk):
        toward = 1 if way == 0 else -1
        block = part(chunk, near_z(-toward * step))
        remote(
            block, block, z_send.at[way, step - 1, chunk], z_recv.at[way, step - 1, chunk],
            r, z_peer(toward),
        ).wait_recv()

    def y_group(step):
        ways = (0,) if step == 0 else (0, 1)
        return [
            (step, way, piece) for piece in (0, 1) for way in ways
            if step == 0 or has(way, step, piece + 1)
        ]

    y_order = [item for step in range(last + 1) for item in y_group(step)]

    def y_place(item):
        step, way, _ = item
        return near_z(-step if way == 0 else step)

    def col_part(item):
        return cols.at[pl.ds(item[2] * half, half), y_place(item)]

    def y_copies(item, from_rows):
        i = y_order.index(item)
        tiles = pl.ds(item[2] * half, half)
        source = rows.at[tiles, side, y_place(item)] if from_rows else col_part(item)
        to = [y_peer(1), y_peer(-1), 2 * y + 1 - core]
        return [
            remote(source, col_part(item), y_send.at[i, n], y_recv.at[i], row, q)
            for n, row in enumerate(to)
        ]

    def each_way(copies, act):
        pl.when(goes_up)(lambda: act(copies[0]))
        pl.when(goes_down)(lambda: act(copies[1]))
        act(copies[2])

    def keep(item):
        i = y_order.index(item)
        tiles = pl.ds(item[2] * half, half)
        buffer = held.at[tiles, y_place(item)]
        return (
            pltpu.make_async_copy(rows.at[tiles, side, y_place(item)], buffer, root_sem.at[0, i]),
            pltpu.make_async_copy(buffer, col_part(item), root_sem.at[1, i]),
        )

    def y_start(item):
        @pl.when(is_root)
        def _():
            each_way(y_copies(item, True), lambda copy: copy.start())
            keep(item)[0].start()

    def event_of(item):
        step, _, piece = item
        return 2 * (step - 1) + piece

    lags = range(1, far)
    events = 2 * last

    def y_relay(now):
        for lag in lags:
            if now < events:
                items = [item for item in y_order if event_of(item) == now - lag]
                if now == 0:
                    items = [item for item in y_order if event_of(item) <= -lag]
            else:
                items = [item for item in y_order if event_of(item) >= events - lag]
            if not items:
                continue

            @pl.when(is_relay & ((away == lag) if lag != far - 1 else (away >= lag)))
            def _(items=items):
                for item in items:
                    copies = y_copies(item, False)
                    copies[2].wait_recv()
                    each_way(copies, lambda copy: copy.start())

    def z_pass(step, chunk):
        for way in (0, 1):
            if has(way, step, chunk):
                z_arrived(way, step, chunk)
                if step < last and has(way, step + 1, chunk):
                    z_send_copy(way, step + 1, chunk).start()
                if chunk:
                    y_start((step, way, chunk - 1))

    for chunk in (0, 1, 2):
        if chunk == 1:
            own.wait()
        if chunk == 2:
            z_pass(1, 0)
        for k in range(1, nx):
            x_copy(chunk, k).wait_recv()
        for way in (0, 1):
            z_send_copy(way, 1, chunk).start()
        if chunk:
            y_start((0, 0, chunk - 1))

    fetch = pltpu.make_async_copy(first, first_held, own_sem.at[3])
    early = main & jnp.logical_not(owner_ring)

    def begin():
        fetch.wait()
        leading = first_held[...].astype(F32).reshape(-1, first.shape[-1]).astype(BF16)
        start_factor(leading, first_noise[...].astype(F32)[:1], work)

    done = 0
    for now in range(events):
        step, chunk = now // 2 + 1, now % 2 + 1
        if now + 2 <= last:
            z_pass(now + 2, 0)
            if now + 2 == last:
                pl.when(main)(fetch.start)
        elif now + 1 == last:
            pl.when(early)(begin)
        else:
            pl.when(early)(functools.partial(eliminate, work, done))
            done += 1
        z_pass(step, chunk)
        y_relay(now)

    @pl.when(main & owner_ring)
    def _():
        begin()
        for piece in range(done):
            eliminate(work, piece)

    @pl.when(main)
    def _():
        for piece in range(done, PIECES):
            eliminate(work, piece)
        inverse[...] = end_factor(work)

    y_relay(events)
    handed = remote(inverse, inverse, share_sem.at[0], share_sem.at[1], 2 * y + 1 - core, q)

    @pl.when(is_root)
    def _():
        for item in y_order:
            take, put = keep(item)
            take.wait()
            put.start()
        for item in y_order:
            keep(item)[1].wait()
            each_way(y_copies(item, True), lambda copy: copy.wait_send())

    @pl.when(is_relay)
    def _():
        for item in y_order:
            each_way(y_copies(item, False), lambda copy: copy.wait_send())

    late = [item for item in y_order if event_of(item) >= events - far]

    @pl.when(is_end)
    def _():
        for item in y_order:
            if item not in late:
                y_copies(item, False)[2].wait_recv()

    pl.when(main)(handed.start)

    @pl.when(is_end)
    def _():
        for item in late:
            y_copies(item, False)[2].wait_recv()

    pl.when(main)(handed.wait_send)
    pl.when(jnp.logical_not(main))(handed.wait_recv)

    @pl.when(is_lead)
    def _():
        for k in range(1, prow):
            for copy in lead(k):
                copy.wait_send()

    for chunk in (0, 1, 2):
        for k in range(1, nx):
            x_copy(chunk, k).wait_send()
        for way in (0, 1):
            for step in range(1, last + 1):
                if has(way, step, chunk):
                    z_send_copy(way, step, chunk).wait_send()


def shards(embeddings, noise_var):
    row_count, col_count = lax.axis_size("prow"), lax.axis_size("pcol")
    nx, nz, ny = 4, col_count // 4, row_count // 2
    row_tiles, _, tile, width = embeddings.shape
    ratio = col_count // row_count
    col_tiles = row_tiles // ratio
    local = jnp.transpose(embeddings[:, 0], (0, 2, 1)).reshape(col_tiles, ratio, width, tile)
    pieces = 2 * nz
    anywhere = pl.BlockSpec(memory_space=pl.ANY)
    vmem = pl.BlockSpec(memory_space=pltpu.VMEM)
    dma = pltpu.SemaphoreType.DMA
    rows, cols, first, first_noise, inverse = pl.pallas_call(
        functools.partial(gather_kernel, (nx, nz, ny)),
        in_specs=[vmem, vmem],
        out_specs=[anywhere, anywhere, anywhere, vmem, vmem],
        out_shape=[
            jax.ShapeDtypeStruct((col_tiles, ratio, nz, nx, width, tile), BF16),
            jax.ShapeDtypeStruct((col_tiles, nz, nx, width, tile), BF16),
            jax.ShapeDtypeStruct((nz, nx, width, tile), BF16),
            jax.ShapeDtypeStruct((row_tiles, tile), BF16),
            jax.ShapeDtypeStruct((tile, tile), F32),
        ],
        scratch_shapes=[
            pltpu.VMEM((col_tiles, nz, nx, width, tile), BF16),
            pltpu.VMEM((nz, nx, width, tile), BF16),
            pltpu.VMEM((tile, tile), F32),
            dma((4,)),
            dma((2, row_count - 1)),
            dma((2,)),
            dma((3, nx - 1)),
            dma((3, nx - 1)),
            dma((2, nz // 2, 3)),
            dma((2, nz // 2, 3)),
            dma((pieces, 3)),
            dma((pieces,)),
            dma((2, pieces)),
            dma((2,)),
        ],
        compiler_params=pltpu.CompilerParams(collective_id=0, has_side_effects=True),
        name="gather",
    )(local, noise_var[:, 0])
    feats = width * col_count
    return finish(
        rows.reshape(row_tiles, feats, tile),
        cols.reshape(col_tiles, feats, tile),
        first.reshape(feats, tile),
        noise_var,
        first_noise,
        inverse,
    )


def finish(rows, cols, first, noise_var, first_noise, inverse):
    row_count, col_count = lax.axis_size("prow"), lax.axis_size("pcol")
    row_tiles, feats, tile = rows.shape
    col_tiles = cols.shape[0]
    noise = noise_var[:, 0]
    group = 2
    share = tile // col_count
    height = group * tile * col_tiles
    schur, shared = pl.pallas_call(
        functools.partial(schur_kernel, row_count, col_count),
        grid=(row_tiles // group,),
        in_specs=[
            pl.BlockSpec((group, feats, tile), lambda i: (i, 0, 0)),
            pl.BlockSpec((col_tiles, feats, tile), lambda i: (0, 0, 0)),
            pl.BlockSpec((feats, tile), lambda i: (0, 0)),
            pl.BlockSpec((row_tiles, tile), lambda i: (0, 0)),
            pl.BlockSpec((row_tiles, tile), lambda i: (0, 0)),
            pl.BlockSpec((tile, tile), lambda i: (0, 0)),
        ],
        out_specs=[
            pl.BlockSpec((height, tile), lambda i: (i, 0)),
            pl.BlockSpec((group * share, tile), lambda i: (i, 0)),
        ],
        out_shape=[
            jax.ShapeDtypeStruct((row_tiles * tile * col_tiles, tile), F32),
            jax.ShapeDtypeStruct((row_tiles * share, tile), F32),
        ],
        scratch_shapes=[
            pltpu.VMEM((feats, col_tiles * tile), BF16),
            pltpu.VMEM((1, col_tiles * tile), F32),
            pltpu.VMEM((col_tiles * tile, 3 * tile), BF16),
            pltpu.VMEM((group * tile, tile), F32),
            pltpu.VMEM((row_tiles, tile), F32),
        ],
        name="schur",
    )(rows, cols, first, noise, first_noise, inverse)
    return (
        schur.reshape(row_tiles, 1, tile, col_tiles, 1, tile),
        shared.reshape(row_tiles, 1, share, tile),
    )


def solution(mesh):
    placed = (P(None, "prow", None, "pcol"), P(None, "prow", None))
    return jax.shard_map(
        shards,
        mesh=mesh,
        in_specs=placed,
        out_specs=(P(None, "prow", None, None, "pcol", None), P(None, "prow", "pcol", None)),
        check_vma=False,
    )
```

```python
import functools

import jax
import jax.numpy as jnp
from jax import lax
from jax.experimental import pallas as pl
from jax.experimental.pallas import tpu as pltpu
from jax.sharding import PartitionSpec as P

F32 = jnp.float32
BF16 = jnp.bfloat16


def feature_squares(block):
    wide = block.astype(F32)
    return jnp.sum(wide * wide, axis=0, keepdims=True)


def down(row):
    tile = row.shape[1]
    return jnp.transpose(jnp.broadcast_to(row, (tile, tile)))


def eye_mask(tile):
    rows = lax.broadcasted_iota(jnp.int32, (tile, tile), 0)
    cols = lax.broadcasted_iota(jnp.int32, (tile, tile), 1)
    return rows == cols


def split3(panel, left):
    high = panel.astype(BF16)
    low = (panel - high.astype(F32)).astype(BF16)
    return jnp.concatenate([high, high, low] if left else [high, low, high], axis=1)


def matmul(left, right):
    return lax.dot_general(left, right, (((1,), (0,)), ((), ())), preferred_element_type=F32)


def matmul_nt(left, right, precision=None):
    return lax.dot_general(
        left, right, (((1,), (1,)), ((), ())), precision=precision, preferred_element_type=F32
    )


PIECES = 8


def start_factor(first, noise, work):
    feats = first.shape[0]
    sq = feature_squares(first)
    dots = matmul(jnp.transpose(first), first)
    gram = jnp.exp((2.0 * dots - (down(sq) + sq)) * (1.0 / feats))
    work[...] = gram + jnp.where(eye_mask(first.shape[1]), noise, 0.0)


def eliminate(work, piece):
    tile = work.shape[1]
    part = tile // PIECES
    base = piece * part
    height = tile - base
    lanes = lax.broadcasted_iota(jnp.int32, (height, tile), 1)
    ids = lax.broadcasted_iota(jnp.int32, (height, tile), 0) + base

    def step(k, carry):
        held = work[base:, :]
        at_k = lanes == k
        pivot = work[pl.ds(k, 1), :]
        here = at_k[:1]
        inv = 1.0 / jnp.sum(jnp.where(here, pivot, 0.0), axis=1, keepdims=True)
        column = jnp.sum(jnp.where(at_k, held, 0.0), axis=1, keepdims=True)
        scaled = jnp.where(here, 1.0, pivot) * inv
        factor = jnp.where(ids > k, column, 0.0)
        cleared = jnp.where(at_k & (ids > k), 0.0, held)
        work[base:, :] = cleared - factor * scaled
        return carry

    lax.fori_loop(base, base + part, step, 0)


def end_factor(work):
    tile = work.shape[1]
    diagonal = eye_mask(tile)
    done = work[...]
    pivots = jnp.sum(jnp.where(diagonal, done, 0.0), axis=1, keepdims=True)
    rows = lax.broadcasted_iota(jnp.int32, (tile, tile), 0)
    cols = lax.broadcasted_iota(jnp.int32, (tile, tile), 1)
    unit = jnp.where(cols < rows, done, jnp.where(diagonal, 1.0, 0.0))
    return unit * (1.0 / jnp.sqrt(pivots))


def schur_kernel(
    row_count, col_count, row_ref, col_ref, first_ref, noise_ref, first_noise_ref, inverse_ref,
    schur_ref, share_ref, wide, col_sq, col_panel, panel, noise_held,
):
    step = pl.program_id(0)
    group, feats, tile = row_ref.shape
    col_tiles = col_ref.shape[0]
    scale = 1.0 / feats
    r, q = lax.axis_index("prow"), lax.axis_index("pcol")
    diagonal = eye_mask(tile)
    first = first_ref[...]
    first_sq = feature_squares(first)
    first_noise = jnp.where(diagonal, first_noise_ref[...].astype(F32)[:1], 0.0)

    def panel_of(samples, sq, leads):
        gram = jnp.exp((2.0 * matmul(samples, first) - (sq + first_sq)) * scale)
        head = gram[:tile] + jnp.where(leads, first_noise, 0.0)
        gram = jnp.concatenate([head, gram[tile:]], axis=0)
        return matmul_nt(gram, inverse_ref[...], lax.Precision.HIGHEST)

    @pl.when(step == 0)
    def _():
        noise_held[...] = noise_ref[...].astype(F32)
        samples, squares = [], []
        for d in range(col_tiles):
            block = col_ref[d]
            place = slice(d * tile, (d + 1) * tile)
            wide[:, place] = block
            sq = feature_squares(block)
            col_sq[:, place] = sq
            samples.append(jnp.transpose(block))
            squares.append(down(sq))
        whole = panel_of(jnp.concatenate(samples), jnp.concatenate(squares), q == 0)
        col_panel[...] = split3(whole, False)

    samples = jnp.concatenate([jnp.transpose(row_ref[t]) for t in range(group)])
    sq = jnp.concatenate([down(feature_squares(row_ref[t])) for t in range(group)])
    rows = panel_of(samples, sq, step * group * row_count + r == 0)
    panel[...] = rows
    dots = matmul(samples, wide[...])
    update = matmul_nt(split3(rows, True), col_panel[...])
    tiles = [step * group + t for t in range(group)]
    noises = [jnp.where(diagonal, noise_held[pl.ds(a, 1), :], 0.0) for a in tiles]
    for d in range(col_tiles):
        place = slice(d * tile, (d + 1) * tile)
        gram = jnp.exp((2.0 * dots[:, place] - (sq + col_sq[:, place])) * scale)
        added = jnp.concatenate([
            jnp.where(a * row_count + r == d * col_count + q, noise, 0.0)
            for a, noise in zip(tiles, noises)
        ])
        schur_ref[pl.ds(d, group * tile, stride=col_tiles), :] = gram + added - update[:, place]
    share = tile // col_count
    share_ref[...] = jnp.concatenate(
        [panel[pl.ds(t * tile + q * share, share), :] for t in range(group)]
    )


def gather_kernel(
    shape, local, noise, rows, cols, first, first_noise, inverse,
    held, first_held, work, own_sem, lead_send, lead_recv, x_send, x_recv, z_send, z_recv, y_send, y_recv, root_sem, share_sem,
):
    nx, nz, ny = shape
    col_tiles, ratio = rows.shape[:2]
    half = col_tiles // 2
    r, q = lax.axis_index("prow"), lax.axis_index("pcol")
    x, z = lax.rem(q, nx), lax.div(q, nx)
    core, y = lax.rem(r, 2), lax.div(r, 2)
    prow, total = 2 * ny, nx * nz
    owner = lax.rem(q, prow)
    side = lax.div(q, prow)
    place = lax.rem(y - lax.div(owner, 2) + ny, ny)
    main = core == lax.rem(owner, 2)
    relay_core = 1 - lax.rem(owner, 2)
    is_root = main & (place == 0)
    is_relay = jnp.logical_not(main) & (place != 0)
    is_end = jnp.logical_not(is_root | is_relay)
    is_lead = r == 0
    far = ny // 2
    away = jnp.minimum(place, ny - place)
    goes_up = place < far
    goes_down = (place == 0) | (place > far + 1)

    def near_z(shift):
        return lax.rem(z + shift + nz, nz)

    def x_peer(k):
        return nx * z + lax.rem(x + k, nx)

    def z_peer(shift):
        return nx * near_z(shift) + x

    def y_peer(shift):
        return 2 * lax.rem(y + shift + ny, ny) + relay_core

    def remote(src, dst, send, recv, row, col):
        return pltpu.make_async_remote_copy(
            src_ref=src, dst_ref=dst, send_sem=send, recv_sem=recv,
            device_id=(row, col), device_id_type=pl.DeviceIdType.MESH,
        )

    barrier = pltpu.get_barrier_semaphore()
    for k in range(1, prow):
        pl.semaphore_signal(
            barrier, device_id=(lax.rem(r + k, prow), q), device_id_type=pl.DeviceIdType.MESH
        )
    peers = [x_peer(k) for k in range(1, nx)] + [z_peer(1), z_peer(-1)]
    for peer in peers:
        pl.semaphore_signal(barrier, device_id=(r, peer), device_id_type=pl.DeviceIdType.MESH)
    pl.semaphore_wait(barrier, prow - 1 + len(peers))

    def lead(k):
        return [
            remote(local.at[0, 0], first.at[z, x], lead_send.at[0, k - 1], lead_recv.at[0], k, q),
            remote(noise, first_noise, lead_send.at[1, k - 1], lead_recv.at[1], k, q),
        ]

    own_lead = [
        pltpu.make_async_copy(local.at[0, 0], first.at[z, x], own_sem.at[1]),
        pltpu.make_async_copy(noise, first_noise, own_sem.at[2]),
    ]

    @pl.when(is_lead)
    def _():
        for k in range(1, prow):
            for copy in lead(k):
                copy.start()
        for copy in own_lead:
            copy.start()

    own = pltpu.make_async_copy(local, rows.at[:, :, z, x], own_sem.at[0])
    own.start()

    def part(chunk, at_z, at_x=None):
        spot = (at_z,) if at_x is None else (at_z, at_x)
        if chunk == 0:
            return first.at[spot]
        tiles = pl.ds((chunk - 1) * half, half)
        return rows.at[(tiles, slice(None), *spot)]

    def x_copy(chunk, k):
        source = part(0, z, x) if chunk == 0 else local.at[pl.ds((chunk - 1) * half, half)]
        return remote(
            source, part(chunk, z, x), x_send.at[chunk, k - 1], x_recv.at[chunk, k - 1], r, x_peer(k)
        )

    for chunk in (1, 2):
        for k in range(1, nx):
            x_copy(chunk, k).start()

    @pl.when(is_lead)
    def _():
        for copy in own_lead:
            copy.wait()

    @pl.when(jnp.logical_not(is_lead))
    def _():
        for copy in lead(1):
            copy.wait_recv()

    for k in range(1, nx):
        x_copy(0, k).start()

    last = nz // 2

    def has(way, step, chunk):
        return step < last or (chunk == 2) == (way == 1)

    def z_send_copy(way, step, chunk):
        toward = 1 if way == 0 else -1
        block = part(chunk, near_z(-toward * (step - 1)))
        return remote(
            block, block, z_send.at[way, step - 1, chunk], z_recv.at[way, step - 1, chunk],
            r, z_peer(toward),
        )

    def z_arrived(way, step, chunk):
        toward = 1 if way == 0 else -1
        block = part(chunk, near_z(-toward * step))
        remote(
            block, block, z_send.at[way, step - 1, chunk], z_recv.at[way, step - 1, chunk],
            r, z_peer(toward),
        ).wait_recv()

    def y_group(step):
        ways = (0,) if step == 0 else (0, 1)
        return [
            (step, way, piece) for piece in (0, 1) for way in ways
            if step == 0 or has(way, step, piece + 1)
        ]

    y_order = [item for step in range(last + 1) for item in y_group(step)]

    def y_place(item):
        step, way, _ = item
        return near_z(-step if way == 0 else step)

    def col_part(item):
        return cols.at[pl.ds(item[2] * half, half), y_place(item)]

    def y_copies(item, from_rows):
        i = y_order.index(item)
        tiles = pl.ds(item[2] * half, half)
        source = rows.at[tiles, side, y_place(item)] if from_rows else col_part(item)
        to = [y_peer(1), y_peer(-1), 2 * y + 1 - core]
        return [
            remote(source, col_part(item), y_send.at[i, n], y_recv.at[i], row, q)
            for n, row in enumerate(to)
        ]

    def each_way(copies, act):
        pl.when(goes_up)(lambda: act(copies[0]))
        pl.when(goes_down)(lambda: act(copies[1]))
        act(copies[2])

    def keep(item):
        i = y_order.index(item)
        tiles = pl.ds(item[2] * half, half)
        buffer = held.at[tiles, y_place(item)]
        return (
            pltpu.make_async_copy(rows.at[tiles, side, y_place(item)], buffer, root_sem.at[0, i]),
            pltpu.make_async_copy(buffer, col_part(item), root_sem.at[1, i]),
        )

    def y_start(item):
        @pl.when(is_root)
        def _():
            each_way(y_copies(item, True), lambda copy: copy.start())
            keep(item)[0].start()

    def event_of(item):
        step, _, piece = item
        return 2 * (step - 1) + piece

    lags = range(1, far)
    events = 2 * last

    def y_relay(now):
        for lag in lags:
            if now < events:
                items = [item for item in y_order if event_of(item) == now - lag]
                if now == 0:
                    items = [item for item in y_order if event_of(item) <= -lag]
            else:
                items = [item for item in y_order if event_of(item) >= events - lag]
            if not items:
                continue

            @pl.when(is_relay & ((away == lag) if lag != far - 1 else (away >= lag)))
            def _(items=items):
                for item in items:
                    copies = y_copies(item, False)
                    copies[2].wait_recv()
                    each_way(copies, lambda copy: copy.start())

    def z_pass(step, chunk):
        for way in (0, 1):
            if has(way, step, chunk):
                z_arrived(way, step, chunk)
                if step < last and has(way, step + 1, chunk):
                    z_send_copy(way, step + 1, chunk).start()
                if chunk:
                    y_start((step, way, chunk - 1))

    for chunk in (0, 1, 2):
        if chunk == 1:
            own.wait()
        if chunk == 2:
            z_pass(1, 0)
        for k in range(1, nx):
            x_copy(chunk, k).wait_recv()
        for way in (0, 1):
            z_send_copy(way, 1, chunk).start()
        if chunk:
            y_start((0, 0, chunk - 1))

    fetch = pltpu.make_async_copy(first, first_held, own_sem.at[3])

    def begin():
        fetch.wait()
        leading = first_held[...].astype(F32).reshape(-1, first.shape[-1]).astype(BF16)
        start_factor(leading, first_noise[...].astype(F32)[:1], work)

    done = 0
    for now in range(events):
        step, chunk = now // 2 + 1, now % 2 + 1
        if now + 2 <= last:
            z_pass(now + 2, 0)
            if now + 2 == last:
                pl.when(main)(fetch.start)
        elif now + 1 == last:
            pl.when(main)(begin)
        else:
            pl.when(main)(functools.partial(eliminate, work, done))
            done += 1
        z_pass(step, chunk)
        y_relay(now)

    @pl.when(main)
    def _():
        for piece in range(done, PIECES):
            eliminate(work, piece)
        inverse[...] = end_factor(work)

    y_relay(events)
    handed = remote(inverse, inverse, share_sem.at[0], share_sem.at[1], 2 * y + 1 - core, q)

    @pl.when(is_root)
    def _():
        for item in y_order:
            take, put = keep(item)
            take.wait()
            put.start()
        for item in y_order:
            keep(item)[1].wait()
            each_way(y_copies(item, True), lambda copy: copy.wait_send())

    @pl.when(is_relay)
    def _():
        for item in y_order:
            each_way(y_copies(item, False), lambda copy: copy.wait_send())

    late = [item for item in y_order if event_of(item) >= events - far]

    @pl.when(is_end)
    def _():
        for item in y_order:
            if item not in late:
                y_copies(item, False)[2].wait_recv()

    pl.when(main)(handed.start)

    @pl.when(is_end)
    def _():
        for item in late:
            y_copies(item, False)[2].wait_recv()

    pl.when(main)(handed.wait_send)
    pl.when(jnp.logical_not(main))(handed.wait_recv)

    @pl.when(is_lead)
    def _():
        for k in range(1, prow):
            for copy in lead(k):
                copy.wait_send()

    for chunk in (0, 1, 2):
        for k in range(1, nx):
            x_copy(chunk, k).wait_send()
        for way in (0, 1):
            for step in range(1, last + 1):
                if has(way, step, chunk):
                    z_send_copy(way, step, chunk).wait_send()


def shards(embeddings, noise_var):
    row_count, col_count = lax.axis_size("prow"), lax.axis_size("pcol")
    nx, nz, ny = 4, col_count // 4, row_count // 2
    row_tiles, _, tile, width = embeddings.shape
    ratio = col_count // row_count
    col_tiles = row_tiles // ratio
    local = jnp.transpose(embeddings[:, 0], (0, 2, 1)).reshape(col_tiles, ratio, width, tile)
    pieces = 2 * nz
    anywhere = pl.BlockSpec(memory_space=pl.ANY)
    vmem = pl.BlockSpec(memory_space=pltpu.VMEM)
    dma = pltpu.SemaphoreType.DMA
    rows, cols, first, first_noise, inverse = pl.pallas_call(
        functools.partial(gather_kernel, (nx, nz, ny)),
        in_specs=[vmem, vmem],
        out_specs=[anywhere, anywhere, anywhere, vmem, vmem],
        out_shape=[
            jax.ShapeDtypeStruct((col_tiles, ratio, nz, nx, width, tile), BF16),
            jax.ShapeDtypeStruct((col_tiles, nz, nx, width, tile), BF16),
            jax.ShapeDtypeStruct((nz, nx, width, tile), BF16),
            jax.ShapeDtypeStruct((row_tiles, tile), BF16),
            jax.ShapeDtypeStruct((tile, tile), F32),
        ],
        scratch_shapes=[
            pltpu.VMEM((col_tiles, nz, nx, width, tile), BF16),
            pltpu.VMEM((nz, nx, width, tile), BF16),
            pltpu.VMEM((tile, tile), F32),
            dma((4,)),
            dma((2, row_count - 1)),
            dma((2,)),
            dma((3, nx - 1)),
            dma((3, nx - 1)),
            dma((2, nz // 2, 3)),
            dma((2, nz // 2, 3)),
            dma((pieces, 3)),
            dma((pieces,)),
            dma((2, pieces)),
            dma((2,)),
        ],
        compiler_params=pltpu.CompilerParams(collective_id=0, has_side_effects=True),
        name="gather",
    )(local, noise_var[:, 0])
    feats = width * col_count
    return finish(
        rows.reshape(row_tiles, feats, tile),
        cols.reshape(col_tiles, feats, tile),
        first.reshape(feats, tile),
        noise_var,
        first_noise,
        inverse,
    )


def finish(rows, cols, first, noise_var, first_noise, inverse):
    row_count, col_count = lax.axis_size("prow"), lax.axis_size("pcol")
    row_tiles, feats, tile = rows.shape
    col_tiles = cols.shape[0]
    noise = noise_var[:, 0]
    group = 2
    share = tile // col_count
    height = group * tile * col_tiles
    schur, shared = pl.pallas_call(
        functools.partial(schur_kernel, row_count, col_count),
        grid=(row_tiles // group,),
        in_specs=[
            pl.BlockSpec((group, feats, tile), lambda i: (i, 0, 0)),
            pl.BlockSpec((col_tiles, feats, tile), lambda i: (0, 0, 0)),
            pl.BlockSpec((feats, tile), lambda i: (0, 0)),
            pl.BlockSpec((row_tiles, tile), lambda i: (0, 0)),
            pl.BlockSpec((row_tiles, tile), lambda i: (0, 0)),
            pl.BlockSpec((tile, tile), lambda i: (0, 0)),
        ],
        out_specs=[
            pl.BlockSpec((height, tile), lambda i: (i, 0)),
            pl.BlockSpec((group * share, tile), lambda i: (i, 0)),
        ],
        out_shape=[
            jax.ShapeDtypeStruct((row_tiles * tile * col_tiles, tile), F32),
            jax.ShapeDtypeStruct((row_tiles * share, tile), F32),
        ],
        scratch_shapes=[
            pltpu.VMEM((feats, col_tiles * tile), BF16),
            pltpu.VMEM((1, col_tiles * tile), F32),
            pltpu.VMEM((col_tiles * tile, 3 * tile), BF16),
            pltpu.VMEM((group * tile, tile), F32),
            pltpu.VMEM((row_tiles, tile), F32),
        ],
        name="schur",
    )(rows, cols, first, noise, first_noise, inverse)
    return (
        schur.reshape(row_tiles, 1, tile, col_tiles, 1, tile),
        shared.reshape(row_tiles, 1, share, tile),
    )


def solution(mesh):
    placed = (P(None, "prow", None, "pcol"), P(None, "prow", None))
    return jax.shard_map(
        shards,
        mesh=mesh,
        in_specs=placed,
        out_specs=(P(None, "prow", None, None, "pcol", None), P(None, "prow", "pcol", None)),
        check_vma=False,
    )
```
